32 devices in a mesh: groups: 2 (over x), sp: 16 (over z, y, core).
Axes of the slice: x: 2, y: 2, z: 4, core: 2. Of those that a mesh axis runs over, the one named last changes fastest.
Arguments:
- fields: bfloat16 [2, 128, 64, 1440], P('groups', 'sp'), parts along dimension 0, may hold values from -6 to 6
- cotangent: bfloat16 [2, 128, 64, 1440], P('groups', None, 'sp'), parts along dimension 0, may hold values from -6 to 6
- ocean_mask: int32 [64, 1440], P('sp'), may hold values 0 or 1
- kernel: float32 [256, 7, 7], P('groups'), parts along dimension 0, may hold values from -0.875 to 0.875
- norm_gain: float32 [256], P('groups'), parts along dimension 0, may hold values from 0.25 to 1.75
- norm_shift: float32 [256], P('groups'), parts along dimension 0, may hold values from -3 to 3
- widen: bfloat16 [256, 256], P('groups'), parts along dimension 0, may hold values from -0.5 to 0.5
- hidden_offset: float32 [512], P('groups'), parts along dimension 0, may hold values from -3 to 3
- narrow: bfloat16 [256, 256], P('groups'), parts along dimension 0, may hold values from -0.375 to 0.375
- output_offset: float32 [256], P('groups'), parts along dimension 0, may hold values from -3 to 3
Outputs:
- updated: bfloat16 [2, 128, 64, 1440], P('groups', None, 'sp'), parts along dimension 0
- fields_grad: bfloat16 [2, 128, 64, 1440], P('groups', 'sp'), parts along dimension 0
- kernel_grad: float32 [256, 7, 7], P(('groups', 'sp')), parts along dimension 0
- widen_grad: float32 [256, 256], P(('groups', 'sp')), parts along dimension 0
- narrow_grad: float32 [256, 256], P(('groups', 'sp')), parts along dimension 0
- gain_grad: float32 [256], P('groups'), parts along dimension 0
- shift_grad: float32 [256], P('groups'), parts along dimension 0
- hidden_grad: float32 [512], P('groups'), parts along dimension 0
- output_grad: float32 [256], P('groups'), parts along dimension 0
The draws below stay inside these ranges and needn't reach their ends.
There are 2 independent parts, one for each index of `groups`. The reference program is written for one: setup_inputs(seed, part) draws one part's arguments, and reference() takes and returns one part's arrays. A program takes and returns all parts, laid end to end along the dimension named above; an argument that names none is the same for every part. Nothing has to cross between parts.
Inputs may be any that keep to these rules, and one draw needn't show every extreme that they name: `ocean_mask`: 1 marks an ocean cell, 0 a land cell.
All inputs are finite; a program needn't handle non-finite values. No bound on the sum of `ocean_mask` on one device may be relied on, other than what follows from the above.
Results may differ from the reference program's by a relative error of at most 0.0064.
Values may be sent and summed in bfloat16 or wider, within the bound.
A program may use at most 128 MiB of HBM per device.

```python
import math
import jax
import jax.numpy as jnp
from jax import lax

C = 128
F = 256
KS = 7
LON = 1440
SAMPLES = 1
ROWS_DEV = 4
LAT = 64


def with_ends(array, stream_key, low, high):
    index_at = [jax.random.randint(jax.random.fold_in(stream_key, axis), (), 0, length) for axis, length in enumerate(array.shape)]
    widest = array.shape.index(max(array.shape))
    beside = index_at[:widest] + [(index_at[widest] + 1) % array.shape[widest]] + index_at[widest + 1:]
    return array.at[tuple(index_at)].set(low).at[tuple(beside)].set(high)


def spiked(result, rng, source, target, blocks, factor):
    owner, partner = [(jnp.arange(result.shape[axis_at]) // (result.shape[axis_at] // blocks)).reshape([-1 if axis == axis_at else 1 for axis in range(result.ndim)]) for axis_at in (source, target)]
    chosen = jax.random.permutation(rng, blocks)[partner]
    strong = (owner == chosen) | (owner == (partner + blocks // 2) % blocks)
    return jnp.where(strong, factor * result, result)


def block_scale(rng, dims, split, least, high):
    factor_of, own = 1.0, jax.random.fold_in(rng, 6)
    for position, parts in split:
        steps = jnp.exp(jax.random.uniform(jax.random.fold_in(own, position), (parts,), jnp.float32, least / len(split), high / len(split)))
        factor_of = factor_of * jnp.repeat(steps, dims[position] // parts).reshape([-1 if axis == position else 1 for axis in range(len(dims))])
    return factor_of


def scatter_about(stream_key, dims, deviation, bound, cuts=(), kind=jnp.bfloat16):
    values = deviation * jax.random.normal(stream_key, dims, jnp.float32)
    if cuts:
        values = values * block_scale(stream_key, dims, cuts, -0.22, 0.18)
    return jnp.clip(values, -bound, bound).astype(kind)


def gaussian_with(key, extent, scale, bound, pieces, heavy, kind=jnp.bfloat16):
    values = scale * jax.random.normal(key, extent, jnp.float32)
    if pieces:
        values = values * block_scale(key, extent, pieces, -0.22, 0.18)
    return jnp.clip(spiked(values, jax.random.fold_in(key, 3), *heavy), -bound, bound).astype(kind)


def setup_inputs(seed: int = 0, part: int = 0) -> dict:
    streams_of = jax.random.split(jax.random.key(seed), 11)
    part_keys = jax.random.split(jax.random.fold_in(streams_of[10], part), 11)
    return {
        "fields": scatter_about(part_keys[0], (SAMPLES, C, LAT, LON), 1.0, 6.0, ((1, 16),)),
        "cotangent": gaussian_with(part_keys[1], (SAMPLES, C, LAT, LON), 1.0, 6.0, ((2, 16),), (2, 1, 16, 2.0)),
        "ocean_mask": with_ends((jax.random.randint(streams_of[2], (LAT, LON), 0, 4) < 3).astype(jnp.int32), jax.random.fold_in(streams_of[2], 1), 0, 1),
        "kernel": scatter_about(part_keys[3], (C, KS, KS), (KS * KS) ** -0.5, 0.875, (), jnp.float32),
        "norm_gain": jnp.clip(1.0 + 0.15 * jax.random.normal(part_keys[4], (C,), jnp.float32), 0.25, 1.75),
        "norm_shift": scatter_about(part_keys[5], (C,), 0.5, 3.0, (), jnp.float32),
        "widen": scatter_about(part_keys[6], (C, F), C ** -0.5, 0.5),
        "hidden_offset": scatter_about(part_keys[7], (F,), 0.5, 3.0, (), jnp.float32),
        "narrow": scatter_about(part_keys[8], (C, F), F ** -0.5, 0.375),
        "output_offset": scatter_about(part_keys[9], (C,), 0.5, 3.0, (), jnp.float32),
    }


EPSILON = 1e-06
PRECISE = lax.Precision.HIGHEST

def product(pattern, former, latter):
    return jnp.einsum(pattern, former.astype(jnp.float32), latter.astype(jnp.float32), precision=PRECISE)

def wrap_lon(values, rim_width):
    return jnp.concatenate([values[..., -rim_width:], values, values[..., :rim_width]], axis=-1)

def wrap_pad(values, rim_width):
    widened = wrap_lon(values, rim_width)
    return jnp.pad(widened, [(0, 0)] * (values.ndim - 2) + [(rim_width, rim_width), (0, 0)])

def apply_taps(padded, kernel_set, rows, cols):
    running = jnp.zeros(padded.shape[:2] + (rows, cols), jnp.float32)
    for row_tap in range(KS):
        for col_tap in range(KS):
            weight = kernel_set[:, row_tap, col_tap][None, :, None, None]
            running = running + weight * padded[:, :, row_tap:row_tap + rows, col_tap:col_tap + cols]
    return running

def tap_grads(padded, grads, rows, cols):
    return jnp.stack([jnp.stack([lax.optimization_barrier(jnp.sum(padded[:, :, row_tap:row_tap + rows, col_tap:col_tap + cols] * grads, axis=(0, 2, 3))) for col_tap in range(KS)], axis=-1) for row_tap in range(KS)], axis=1)

def gelu_slope(hidden):
    cdf = 0.5 * (1.0 + jax.scipy.special.erf(hidden * (1.0 / math.sqrt(2.0))))
    return cdf + hidden * jnp.exp(-0.5 * hidden * hidden) * (1.0 / math.sqrt(2.0 * math.pi))

def pointwise(conv_out, fields, cotangent, mask_rows, params):
    norm_gain, norm_shift, widen, hidden_offset, narrow, output_offset = params
    values = conv_out.astype(jnp.float32)
    centre = lax.optimization_barrier(jnp.mean(values, axis=1, keepdims=True))
    centred = values - centre
    inv_std = lax.rsqrt(lax.optimization_barrier(jnp.mean(centred * centred, axis=1, keepdims=True)) + EPSILON)
    normed = centred * inv_std
    scaled = (normed * norm_gain[None, :, None, None] + norm_shift[None, :, None, None]).astype(jnp.bfloat16)
    hidden = product('schw,cf->sfhw', scaled, widen) + hidden_offset[None, :, None, None]
    active = jax.nn.gelu(hidden, approximate=False).astype(jnp.bfloat16)
    branch = product('sfhw,cf->schw', active, narrow) + output_offset[None, :, None, None]
    ocean_rows = mask_rows.astype(jnp.float32)[None, None]
    updated = (fields.astype(jnp.float32) + ocean_rows * branch).astype(jnp.bfloat16)
    upstream = (cotangent.astype(jnp.float32) * ocean_rows).astype(jnp.bfloat16)
    output_part = lax.optimization_barrier(jnp.sum(upstream.astype(jnp.float32), axis=(0, 2, 3)))
    narrow_part = product('schw,sfhw->cf', upstream, active)
    active_back = product('schw,cf->sfhw', upstream, narrow)
    hidden_back = (active_back * gelu_slope(hidden)).astype(jnp.bfloat16)
    hidden_part = lax.optimization_barrier(jnp.sum(hidden_back.astype(jnp.float32), axis=(0, 2, 3)))
    widen_part = product('schw,sfhw->cf', scaled, hidden_back)
    scaled_back = product('sfhw,cf->schw', hidden_back, widen)
    gain_part = lax.optimization_barrier(jnp.sum(scaled_back * normed, axis=(0, 2, 3)))
    shift_part = lax.optimization_barrier(jnp.sum(scaled_back, axis=(0, 2, 3)))
    normed_back = scaled_back * norm_gain[None, :, None, None]
    conv_back = inv_std * (normed_back - lax.optimization_barrier(jnp.mean(normed_back, axis=1, keepdims=True)) - normed * lax.optimization_barrier(jnp.mean(normed_back * normed, axis=1, keepdims=True)))
    return (updated, conv_back.astype(jnp.bfloat16), (widen_part, narrow_part, gain_part, shift_part, hidden_part, output_part))

def reference(fields, cotangent, ocean_mask, kernel, norm_gain, norm_shift, widen, hidden_offset, narrow, output_offset):
    params = (norm_gain, norm_shift, widen, hidden_offset, narrow, output_offset)
    rim_width = KS // 2
    grad_scale = 1.0 / math.sqrt(SAMPLES * LAT * LON)
    by_channel = jnp.moveaxis(fields, 1, 0)

    def forward_conv(inputs):
        channel_plane, kernel_one = inputs
        padded = wrap_pad(channel_plane[:, None].astype(jnp.float32), rim_width)
        return apply_taps(padded, kernel_one[None], LAT, LON)[:, 0].astype(jnp.bfloat16)
    conv_out = jnp.moveaxis(lax.map(forward_conv, (by_channel, kernel)), 0, 1)
    blocks = LAT // ROWS_DEV

    def one_block(totals, block_index):
        first_row = (block_index * ROWS_DEV).astype(jnp.int32)

        def take_rows(source):
            return lax.dynamic_slice_in_dim(source, first_row, ROWS_DEV, 2)
        mask_rows = lax.dynamic_slice_in_dim(ocean_mask, first_row, ROWS_DEV, 0)
        updated, conv_back, partials = pointwise(take_rows(conv_out), take_rows(fields), take_rows(cotangent), mask_rows, params)
        return (tuple((running + extra for running, extra in zip(totals, partials))), (updated, conv_back))
    starts = (jnp.zeros((C, F), jnp.float32), jnp.zeros((C, F), jnp.float32), jnp.zeros((C,), jnp.float32), jnp.zeros((C,), jnp.float32), jnp.zeros((F,), jnp.float32), jnp.zeros((C,), jnp.float32))
    totals, (updated_blocks, back_blocks) = lax.scan(one_block, starts, jnp.arange(blocks, dtype=jnp.int32))
    updated = jnp.moveaxis(updated_blocks, 0, 2).reshape(SAMPLES, C, LAT, LON)
    conv_back = jnp.moveaxis(back_blocks, 0, 2).reshape(SAMPLES, C, LAT, LON)

    def backward_conv(inputs):
        channel_plane, grad_plane, upstream_plane, kernel_one = inputs
        padded = wrap_pad(channel_plane[:, None].astype(jnp.float32), rim_width)
        grad_values = grad_plane[:, None].astype(jnp.float32)
        kernel_part = tap_grads(padded, grad_values, LAT, LON)[0]
        spread = apply_taps(wrap_pad(grad_values, rim_width), kernel_one[None, ::-1, ::-1], LAT, LON)[:, 0]
        return (kernel_part, (upstream_plane.astype(jnp.float32) + spread).astype(jnp.bfloat16))
    kernel_sum, grad_planes = lax.map(backward_conv, (by_channel, jnp.moveaxis(conv_back, 1, 0), jnp.moveaxis(cotangent, 1, 0), kernel))
    fields_grad = jnp.moveaxis(grad_planes, 0, 1)
    widen_sum, narrow_sum, gain_sum, shift_sum, hidden_sum, output_sum = totals
    return (updated, fields_grad, kernel_sum * grad_scale, widen_sum * grad_scale, narrow_sum * grad_scale, gain_sum * grad_scale, shift_sum * grad_scale, hidden_sum * grad_scale, output_sum * grad_scale)
```

```python
import functools
import math

import jax
import jax.numpy as jnp
import numpy as np
from jax import lax
from jax.experimental import pallas as pl
from jax.experimental.pallas import tpu as pltpu
from jax.sharding import PartitionSpec as P

KS = 7
RIM = KS // 2
EPSILON = 1e-06
GROUP = 16
NT = (((1,), (1,)), ((), ()))


def dot(former, latter):
    return jnp.dot(former, latter, preferred_element_type=jnp.float32)


def dot_nt(former, latter):
    return lax.dot_general(former, latter, NT, preferred_element_type=jnp.float32)


def band_matrix(kernel, rows):
    channels = kernel.shape[0]
    taps = jnp.swapaxes(kernel, 1, 2)
    shifted = jnp.stack([jnp.pad(taps, ((0, 0), (0, 0), (h, rows - 1 - h))) for h in range(rows)])
    span = KS * (rows + KS - 1)
    shifted = shifted.reshape(rows, channels, span).astype(jnp.bfloat16)
    spread = jnp.asarray(np.repeat(np.eye(span, dtype=np.float32), GROUP, axis=1), jnp.bfloat16)
    wide = jnp.einsum("hck,kn->hcn", shifted, spread, preferred_element_type=jnp.float32)
    same = (jnp.arange(channels)[:, None] % GROUP) == (jnp.arange(span * GROUP)[None, :] % GROUP)
    return jnp.where(same[None], wide, 0.0).astype(jnp.bfloat16)


def shifts(values, scratch):
    rows, group, lon = values.shape
    flat = values.reshape(rows * group, lon)
    wrapped = jnp.concatenate([flat[:, -RIM:], flat, flat[:, :RIM]], axis=1)
    for tap in range(KS):
        scratch[tap * rows * group : (tap + 1) * rows * group, :] = wrapped[:, tap : tap + lon]


def conv_kernel(above, own, below, band, out, scratch):
    rows, group, lon = own.shape
    shifts(jnp.concatenate([above[:, :, :lon], own[...], below[:, :, :lon]], axis=0), scratch)
    result = dot(band[...].reshape(rows * group, -1), scratch[...])
    out[...] = result.astype(out.dtype).reshape(rows, group, lon)


def tap_kernel(above, own, below, grads, parts, scratch):
    rows, group, lon = own.shape
    shifts(jnp.concatenate([above[:, :, :lon], own[...], below[:, :, :lon]], axis=0), scratch)
    pairs = dot_nt(grads[...].reshape(rows * group, lon), scratch[...])
    row = lax.broadcasted_iota(jnp.int32, pairs.shape, 0) % group
    col = lax.broadcasted_iota(jnp.int32, pairs.shape, 1) % group
    kept = jnp.where(row == col, pairs, 0.0)
    total = jnp.sum(kept[:group], axis=0, keepdims=True)
    for h in range(1, rows):
        line = jnp.sum(kept[h * group : (h + 1) * group], axis=0, keepdims=True)
        total += jnp.concatenate([line[:, h * group :], line[:, : h * group]], axis=1)
    parts[...] = total[None]


def back_kernel(above, own, below, cotangent, band, out, scratch):
    rows, group, lon = own.shape
    shifts(jnp.concatenate([above[:, :, :lon], own[...], below[:, :, :lon]], axis=0), scratch)
    spread = dot(band[...].reshape(rows * group, -1), scratch[...])
    total = cotangent[...].reshape(rows * group, lon).astype(jnp.float32) + spread
    out[...] = total.astype(out.dtype).reshape(rows, group, lon)


def pointwise_kernel(
    conv, fields, cotangent, mask, gain, shift, widen, widen_t, hidden_off, narrow, narrow_t, out_off,
    updated, conv_back, widen_part, narrow_part, gain_part, shift_part, hidden_part, out_part,
):
    lon = conv.shape[-1]

    @pl.when(pl.program_id(0) == 0)
    def _():
        for part in (widen_part, narrow_part, gain_part, shift_part, hidden_part, out_part):
            part[...] = jnp.zeros_like(part)

    f32, bf16 = jnp.float32, jnp.bfloat16
    step = 256
    for first in range(0, lon, step):
        cols = slice(first, min(first + step, lon))
        values = conv[0, :, cols].astype(f32)
        centre = jnp.mean(values, axis=0, keepdims=True)
        centred = values - centre
        inv_std = lax.rsqrt(jnp.mean(centred * centred, axis=0, keepdims=True) + EPSILON)
        normed = centred * inv_std
        scaled = (normed * gain[...] + shift[...]).astype(bf16)
        hidden = dot(widen_t[...], scaled) + hidden_off[...]
        cdf = 0.5 * (1.0 + lax.erf(hidden * (1.0 / math.sqrt(2.0))))
        active = (hidden * cdf).astype(bf16)
        slope = cdf + hidden * jnp.exp(-0.5 * hidden * hidden) * (1.0 / math.sqrt(2.0 * math.pi))
        ocean = mask[0, :, cols].astype(f32)
        branch = dot(narrow[...], active) + out_off[...]
        updated[0, :, cols] = (fields[0, :, cols].astype(f32) + ocean * branch).astype(bf16)
        upstream_wide = cotangent[0, :, cols].astype(f32) * ocean
        upstream = upstream_wide.astype(bf16)
        out_part[...] += jnp.sum(upstream_wide, axis=1, keepdims=True)
        narrow_part[...] += dot_nt(upstream, active)
        hidden_wide = dot(narrow_t[...], upstream) * slope
        hidden_back = hidden_wide.astype(bf16)
        hidden_part[...] += jnp.sum(hidden_wide, axis=1, keepdims=True)
        widen_part[...] += dot_nt(scaled, hidden_back)
        scaled_back = dot(widen[...], hidden_back)
        gain_part[...] += jnp.sum(scaled_back * normed, axis=1, keepdims=True)
        shift_part[...] += jnp.sum(scaled_back, axis=1, keepdims=True)
        normed_back = scaled_back * gain[...]
        conv_back[0, :, cols] = (
            inv_std
            * (
                normed_back
                - jnp.mean(normed_back, axis=0, keepdims=True)
                - normed * jnp.mean(normed_back * normed, axis=0, keepdims=True)
            )
        ).astype(bf16)


def halos(values, devices):
    def send(piece, pairs):
        piece = jnp.pad(piece, ((0, 0), (0, 0), (0, -piece.shape[2] % 128)))
        return lax.ppermute(piece, "sp", pairs)

    above = send(values[-RIM:], [(d, d + 1) for d in range(devices - 1)])
    below = send(values[:RIM], [(d + 1, d) for d in range(devices - 1)])
    return above, below


MESH = pl.DeviceIdType.MESH
LAG = 3


def eye_of(length):
    return lax.broadcasted_iota(jnp.int32, (length, length), 0) == lax.broadcasted_iota(
        jnp.int32, (length, length), 1
    )


def to_column(line):
    return jnp.sum(jnp.where(eye_of(line.shape[1]), line, 0.0), axis=1, keepdims=True)


def to_line(column):
    return jnp.sum(jnp.where(eye_of(column.shape[0]), column, 0.0), axis=0, keepdims=True)


def reorder(a, b, c):
    size = a * b * c
    out = lax.broadcasted_iota(jnp.int32, (size, size), 0)
    col = lax.broadcasted_iota(jnp.int32, (size, size), 1)
    source = ((out // c) % a) * (b * c) + (out // (a * c)) * c + out % c
    return jnp.where(source == col, 1.0, 0.0).astype(jnp.bfloat16)


def tap_spread(row, rows, flip):
    lines = rows + KS - 1
    span = KS * lines * GROUP
    tap = lax.broadcasted_iota(jnp.int32, (64, span), 0)
    col = lax.broadcasted_iota(jnp.int32, (64, span), 1)
    shift, line = col // (lines * GROUP), (col // GROUP) % lines
    i = line - row
    wanted = i * KS + shift
    if flip:
        wanted = KS * KS - 1 - wanted
    return jnp.where((i >= 0) & (i < KS) & (tap == wanted), 1.0, 0.0).astype(jnp.bfloat16)


def block_kernel(
    fields, cot, mask, taps, gain_line, shift_line, widen, widen_t, hidden_line, narrow, narrow_t, out_line,
    updated, fields_grad, weight_sum, rest_sum,
    send, recv, own, above, below, band, band_back, shifted, conv_out, conv_back, g_above, g_below, osend, orecv,
    weight_part, weight_recv, rest_part, rest_recv, pairs,
    gain, shift, hidden_off, out_off, gain_part, shift_part, hidden_part, out_part,
    f_send, f_recv, h_send, h_recv, c_send, c_recv, o_send, o_recv, w_send, w_recv, t_send, t_recv, local_sem,
    *, devices,
):
    f32, bf16 = jnp.float32, jnp.bfloat16
    me = lax.axis_index("sp")
    rows, channels, lon = own.shape
    own_ch = fields.shape[0]
    wide = widen.shape[1]
    groups = channels // GROUP
    per_group = GROUP // own_ch
    lines = rows * own_ch
    tall = GROUP // rows
    span = band.shape[1]
    grad_scale = 1.0 / math.sqrt(rows * devices * lon)

    def loop(first, last, body):
        def step(k, carry):
            body(k)
            return carry

        lax.fori_loop(first, last, step, 0)

    def copy(source, target, s_sem, r_sem, device):
        return pltpu.make_async_remote_copy(
            src_ref=source, dst_ref=target, send_sem=s_sem, recv_sem=r_sem,
            device_id={"sp": device}, device_id_type=MESH,
        )

    def lanes_of(g):
        return pl.ds(pl.multiple_of(g * GROUP, GROUP), GROUP)

    barrier = pltpu.get_barrier_semaphore()
    loop(1, devices, lambda k: pl.semaphore_signal(
        barrier, inc=1, device_id={"sp": lax.rem(me + k, devices)}, device_id_type=MESH))
    pl.semaphore_wait(barrier, devices - 1)

    def f_copy(block, target):
        return copy(send.at[target], recv.at[block], f_send.at[target], f_recv.at[block], target)

    to_blocks = reorder(own_ch, tall * rows, 1)
    turns = devices // tall

    def pack(k):
        part = lax.rem(me // tall + k, turns)
        piece = fields[:, pl.ds(pl.multiple_of(part * GROUP, GROUP), GROUP), :].reshape(own_ch * GROUP, lon)
        moved = dot(to_blocks, piece).astype(bf16)
        send[pl.ds(part * tall, tall)] = moved.reshape(tall, lines, lon)
        for t in range(tall):
            target = part * tall + t

            @pl.when(target != me)
            def _():
                f_copy(me, target).start()

    loop(0, turns, pack)
    keep = pltpu.make_async_copy(send.at[me], recv.at[me], local_sem.at[0])
    keep.start()

    weights = taps[...].astype(bf16)
    same = (lax.broadcasted_iota(jnp.int32, (channels, span), 0) % GROUP) == (
        lax.broadcasted_iota(jnp.int32, (channels, span), 1) % GROUP
    )
    for h in range(rows):
        for flip, result in ((False, band), (True, band_back)):
            full = jnp.where(same, dot(weights, tap_spread(h, rows, flip)), 0.0).astype(bf16)
            for g in range(groups):
                first = (g * rows + h) * GROUP
                result[first : first + GROUP, :] = full[g * GROUP : (g + 1) * GROUP]
    gain[...] = to_column(gain_line[...])
    shift[...] = to_column(shift_line[...])
    hidden_off[...] = to_column(hidden_line[...])
    out_off[...] = to_column(out_line[...])
    for part in (weight_part, rest_part, gain_part, shift_part, hidden_part, out_part):
        part[...] = jnp.zeros_like(part)

    @pl.when(me == 0)
    def _():
        above[...] = jnp.zeros_like(above)
        g_above[...] = jnp.zeros_like(g_above)

    @pl.when(me == devices - 1)
    def _():
        below[...] = jnp.zeros_like(below)
        g_below[...] = jnp.zeros_like(g_below)

    keep.wait()

    def down_copy(g):
        return copy(own.at[rows - RIM : rows, lanes_of(g), :], above.at[:, lanes_of(g), :],
                    h_send.at[g], h_recv.at[g], me + 1)

    def up_copy(g):
        return copy(own.at[0:RIM, lanes_of(g), :], below.at[:, lanes_of(g), :],
                    h_send.at[groups + g], h_recv.at[groups + g], me - 1)

    to_rows = reorder(per_group, rows, own_ch)
    to_owners = reorder(rows, per_group, own_ch)
    my_group = me // per_group

    def group_at(k):
        return lax.rem(my_group + groups - k, groups)

    def receive(g):
        for t in range(per_group):
            source = g * per_group + t

            @pl.when(source != me)
            def _():
                f_copy(source, source).wait_recv()

        pair = recv[pl.ds(g * per_group, per_group)].reshape(per_group * lines, lon)
        own[:, lanes_of(g), :] = dot(to_rows, pair).astype(bf16).reshape(rows, GROUP, lon)

        @pl.when(me < devices - 1)
        def _():
            down_copy(g).start()

        @pl.when(me > 0)
        def _():
            up_copy(g).start()

    def conv(g):
        @pl.when(me > 0)
        def _():
            copy(above.at[:, lanes_of(g), :], above.at[:, lanes_of(g), :],
                 h_send.at[g], h_recv.at[g], me - 1).wait_recv()

        @pl.when(me < devices - 1)
        def _():
            copy(below.at[:, lanes_of(g), :], below.at[:, lanes_of(g), :],
                 h_send.at[groups + g], h_recv.at[groups + g], me + 1).wait_recv()

        shifts(jnp.concatenate([above[:, lanes_of(g), :], own[:, lanes_of(g), :], below[:, lanes_of(g), :]], axis=0),
               shifted)
        taken = band[pl.ds(pl.multiple_of(g * rows * GROUP, rows * GROUP), rows * GROUP), :]
        conv_out[:, lanes_of(g), :] = dot(taken, shifted[...]).astype(bf16).reshape(rows, GROUP, lon)

    def forward(k):
        @pl.when(k < groups)
        def _():
            receive(group_at(k))

        @pl.when(k >= LAG)
        def _():
            conv(group_at(lax.rem(k - LAG + 1, groups)))

    loop(0, groups + LAG, forward)

    def row_down(r):
        return copy(conv_back.at[r], g_above.at[r - (rows - RIM)], c_send.at[r], c_recv.at[r], me + 1)

    def row_up(r):
        return copy(conv_back.at[r], g_below.at[r], c_send.at[rows + r], c_recv.at[rows + r], me - 1)

    def pointwise(r):
        step = 256
        for first in range(0, lon, step):
            cols = slice(first, min(first + step, lon))
            values = conv_out[r, :, cols].astype(f32)
            centre = jnp.mean(values, axis=0, keepdims=True)
            centred = values - centre
            inv_std = lax.rsqrt(jnp.mean(centred * centred, axis=0, keepdims=True) + EPSILON)
            normed = centred * inv_std
            scaled = (normed * gain[...] + shift[...]).astype(bf16)
            hidden = dot(widen_t[...], scaled) + hidden_off[...]
            cdf = 0.5 * (1.0 + lax.erf(hidden * (1.0 / math.sqrt(2.0))))
            active = (hidden * cdf).astype(bf16)
            slope = cdf + hidden * jnp.exp(-0.5 * hidden * hidden) * (1.0 / math.sqrt(2.0 * math.pi))
            ocean = mask[pl.ds(r, 1), cols].astype(f32)
            branch = dot(narrow[...], active) + out_off[...]
            updated[r, :, cols] = (own[r, :, cols].astype(f32) + ocean * branch).astype(bf16)
            upstream_wide = cot[r, :, cols].astype(f32) * ocean
            upstream = upstream_wide.astype(bf16)
            out_part[...] += jnp.sum(upstream_wide, axis=1, keepdims=True)
            weight_part[:, wide:] += dot_nt(upstream, active)
            hidden_wide = dot(narrow_t[...], upstream) * slope
            hidden_back = hidden_wide.astype(bf16)
            hidden_part[...] += jnp.sum(hidden_wide, axis=1, keepdims=True)
            weight_part[:, :wide] += dot_nt(scaled, hidden_back)
            scaled_back = dot(widen[...], hidden_back)
            gain_part[...] += jnp.sum(scaled_back * normed, axis=1, keepdims=True)
            shift_part[...] += jnp.sum(scaled_back, axis=1, keepdims=True)
            normed_back = scaled_back * gain[...]
            conv_back[r, :, cols] = (
                inv_std
                * (
                    normed_back
                    - jnp.mean(normed_back, axis=0, keepdims=True)
                    - normed * jnp.mean(normed_back * normed, axis=0, keepdims=True)
                )
            ).astype(bf16)

        @pl.when((r >= rows - RIM) & (me < devices - 1))
        def _():
            row_down(r).start()

        @pl.when((r < RIM) & (me > 0))
        def _():
            row_up(r).start()

    loop(0, rows, pointwise)

    def w_copy(block, target):
        return copy(weight_part.at[pl.ds(pl.multiple_of(target * own_ch, own_ch), own_ch), :],
                    weight_recv.at[block], w_send.at[target], w_recv.at[block], target)

    def others(body):
        loop(1, devices, lambda k: body(lax.rem(me + k, devices)))

    others(lambda d: w_copy(me, d).start())

    diagonal = (lax.broadcasted_iota(jnp.int32, (rows * GROUP, span), 0) % GROUP) == (
        lax.broadcasted_iota(jnp.int32, (rows * GROUP, span), 1) % GROUP
    )

    def tap(g):
        shifts(jnp.concatenate([above[:, lanes_of(g), :], own[:, lanes_of(g), :], below[:, lanes_of(g), :]], axis=0),
               shifted)
        found = dot_nt(conv_back[:, lanes_of(g), :].reshape(rows * GROUP, lon), shifted[...])
        pairs[:, lanes_of(g), :] = jnp.where(diagonal, found, 0.0).reshape(rows, GROUP, span)

    def o_copy(block, target):
        return copy(osend.at[target], orecv.at[block], o_send.at[target], o_recv.at[block], target)

    def back(g):
        shifts(jnp.concatenate([g_above[:, lanes_of(g), :], conv_back[:, lanes_of(g), :], g_below[:, lanes_of(g), :]],
                               axis=0), shifted)
        taken = band_back[pl.ds(pl.multiple_of(g * rows * GROUP, rows * GROUP), rows * GROUP), :]
        total = cot[:, lanes_of(g), :].reshape(rows * GROUP, lon).astype(f32) + dot(taken, shifted[...])
        moved = dot(to_owners, total.astype(bf16)).astype(bf16)
        osend[pl.ds(g * per_group, per_group)] = moved.reshape(per_group, lines, lon)
        for t in range(per_group):
            target = g * per_group + t

            @pl.when(target != me)
            def _():
                o_copy(me, target).start()

    loop(0, LAG, tap)
    for r in range(rows):
        @pl.when((r >= rows - RIM) & (me > 0))
        def _(r=r):
            copy(g_above.at[max(r - (rows - RIM), 0)], g_above.at[max(r - (rows - RIM), 0)],
                 c_send.at[r], c_recv.at[r], me - 1).wait_recv()

        @pl.when((r < RIM) & (me < devices - 1))
        def _(r=r):
            copy(g_below.at[min(r, RIM - 1)], g_below.at[min(r, RIM - 1)],
                 c_send.at[rows + r], c_recv.at[rows + r], me + 1).wait_recv()

    loop(0, groups, lambda k: back(lax.rem(my_group + groups // 2 + k, groups)))
    own_back = pltpu.make_async_copy(osend.at[me], orecv.at[me], local_sem.at[1])
    own_back.start()
    loop(LAG, groups, tap)

    found = jnp.zeros((channels, 64), f32)
    for h in range(rows):
        spread = tap_spread(h, rows, False)
        exact = pairs[h]
        high = exact.astype(bf16)
        low = (exact - high.astype(f32)).astype(bf16)
        found = found + dot_nt(high, spread) + dot_nt(low, spread)
    rest_part[:, :64] = found
    small = jnp.concatenate(
        [to_line(gain_part[...]), to_line(shift_part[...])]
        + [to_line(hidden_part[first : first + 128]) for first in range(0, wide, 128)]
        + [to_line(out_part[...])], axis=0)
    for d in range(devices):
        rest_part[d * own_ch : d * own_ch + small.shape[0], 128:] = small

    def t_copy(block, target):
        return copy(rest_part.at[pl.ds(pl.multiple_of(target * own_ch, own_ch), own_ch), :],
                    rest_recv.at[block], t_send.at[target], t_recv.at[block], target)

    others(lambda d: t_copy(me, d).start())

    own_back.wait()
    from_blocks = reorder(tall * rows, own_ch, 1)

    def unpack(k):
        part = lax.rem(me // tall + k, turns)
        for t in range(tall):
            source = part * tall + t

            @pl.when(source != me)
            def _():
                o_copy(source, source).wait_recv()

        piece = orecv[pl.ds(part * tall, tall)].reshape(tall * lines, lon)
        fields_grad[:, pl.ds(pl.multiple_of(part * GROUP, GROUP), GROUP), :] = (
            dot(from_blocks, piece).astype(bf16).reshape(own_ch, GROUP, lon)
        )

    loop(0, turns, unpack)

    mine = pl.ds(pl.multiple_of(me * own_ch, own_ch), own_ch)
    weight_recv[pl.ds(me, 1)] = weight_part[mine, :][None]
    rest_recv[pl.ds(me, 1)] = rest_part[mine, :][None]
    others(lambda d: w_copy(d, d).wait_recv())
    others(lambda d: t_copy(d, d).wait_recv())
    weight_sum[...] = jnp.sum(weight_recv[...], axis=0) * grad_scale
    rest_sum[...] = jnp.sum(rest_recv[...], axis=0) * grad_scale

    others(lambda d: f_copy(me, d).wait_send())
    others(lambda d: o_copy(me, d).wait_send())
    others(lambda d: w_copy(me, d).wait_send())
    others(lambda d: t_copy(me, d).wait_send())

    @pl.when(me < devices - 1)
    def _():
        loop(0, groups, lambda g: down_copy(g).wait_send())
        loop(rows - RIM, rows, lambda r: row_down(r).wait_send())

    @pl.when(me > 0)
    def _():
        loop(0, groups, lambda g: up_copy(g).wait_send())
        loop(0, RIM, lambda r: row_up(r).wait_send())


def fused(
    fields, cotangent, ocean_mask, kernel, norm_gain, norm_shift, widen, hidden_offset, narrow, output_offset
):
    devices = lax.axis_size("sp")
    _, channels, rows, lon = cotangent.shape
    own_ch = channels // devices
    wide = widen.shape[1]
    groups = channels // GROUP
    span = KS * (rows + KS - 1) * GROUP
    f32, bf16 = jnp.float32, jnp.bfloat16
    cot_rows = jnp.swapaxes(cotangent[0], 0, 1)
    taps = jnp.pad(kernel.reshape(channels, KS * KS), ((0, 0), (0, 64 - KS * KS)))
    line = lambda vector: vector[None, :]
    vmem = pl.BlockSpec(memory_space=pltpu.VMEM)
    dma = pltpu.SemaphoreType.DMA
    updated, fields_grad, weight_sum, rest_sum = pl.pallas_call(
        functools.partial(block_kernel, devices=devices),
        name="block",
        in_specs=[vmem] * 12,
        out_specs=[vmem] * 4,
        out_shape=[
            jax.ShapeDtypeStruct((rows, channels, lon), bf16),
            jax.ShapeDtypeStruct((own_ch, rows * devices, lon), bf16),
            jax.ShapeDtypeStruct((own_ch, 2 * wide), f32),
            jax.ShapeDtypeStruct((own_ch, 256), f32),
        ],
        scratch_shapes=[
            pltpu.VMEM((devices, rows * own_ch, lon), bf16),
            pltpu.VMEM((devices, rows * own_ch, lon), bf16),
            pltpu.VMEM((rows, channels, lon), bf16),
            pltpu.VMEM((RIM, channels, lon), bf16),
            pltpu.VMEM((RIM, channels, lon), bf16),
            pltpu.VMEM((groups * rows * GROUP, span), bf16),
            pltpu.VMEM((groups * rows * GROUP, span), bf16),
            pltpu.VMEM((span, lon), bf16),
            pltpu.VMEM((rows, channels, lon), bf16),
            pltpu.VMEM((rows, channels, lon), bf16),
            pltpu.VMEM((RIM, channels, lon), bf16),
            pltpu.VMEM((RIM, channels, lon), bf16),
            pltpu.VMEM((devices, rows * own_ch, lon), bf16),
            pltpu.VMEM((devices, rows * own_ch, lon), bf16),
            pltpu.VMEM((channels, 2 * wide), f32),
            pltpu.VMEM((devices, own_ch, 2 * wide), f32),
            pltpu.VMEM((channels, 256), f32),
            pltpu.VMEM((devices, own_ch, 256), f32),
            pltpu.VMEM((rows, channels, span), f32),
            pltpu.VMEM((channels, 1), f32),
            pltpu.VMEM((channels, 1), f32),
            pltpu.VMEM((wide, 1), f32),
            pltpu.VMEM((channels, 1), f32),
            pltpu.VMEM((channels, 1), f32),
            pltpu.VMEM((channels, 1), f32),
            pltpu.VMEM((wide, 1), f32),
            pltpu.VMEM((channels, 1), f32),
            dma((devices,)), dma((devices,)),
            dma((2 * groups,)), dma((2 * groups,)),
            dma((2 * rows,)), dma((2 * rows,)),
            dma((devices,)), dma((devices,)),
            dma((devices,)), dma((devices,)),
            dma((devices,)), dma((devices,)),
            dma((2,)),
        ],
        compiler_params=pltpu.CompilerParams(
            collective_id=0, has_side_effects=True, vmem_limit_bytes=56 * 1024 * 1024
        ),
        cost_estimate=pl.CostEstimate(
            flops=6 * rows * GROUP * span * lon * groups, bytes_accessed=12 * rows * channels * lon,
            transcendentals=0,
        ),
    )(
        fields[0], cot_rows, ocean_mask, taps, line(norm_gain), line(norm_shift), widen, widen.T,
        line(hidden_offset), narrow, narrow.T, line(output_offset),
    )
    small = rest_sum[:, 128:]
    hidden_lines = wide // 128
    return (
        jnp.swapaxes(updated, 0, 1)[None],
        fields_grad[None],
        rest_sum[:, : KS * KS].reshape(own_ch, KS, KS),
        weight_sum[:, :wide],
        weight_sum[:, wide:],
        small[0],
        small[1],
        small[2 : 2 + hidden_lines].reshape(wide),
        small[2 + hidden_lines],
    )


def stepwise(
    fields, cotangent, ocean_mask, kernel, norm_gain, norm_shift, widen, hidden_offset, narrow, output_offset
):
    devices = lax.axis_size("sp")
    samples, channels, rows, lon = cotangent.shape
    wide = widen.shape[1]
    f32, bf16 = jnp.float32, jnp.bfloat16
    grad_scale = 1.0 / math.sqrt(samples * rows * devices * lon)
    groups = channels // GROUP
    span = KS * (rows + KS - 1) * GROUP
    cost = pl.CostEstimate(
        flops=20 * rows * GROUP * span * lon * groups, bytes_accessed=4 * rows * channels * lon * 3, transcendentals=0
    )
    params = pltpu.CompilerParams(vmem_limit_bytes=48 * 1024 * 1024)

    band = band_matrix(kernel, rows)
    band_back = band_matrix(kernel[:, ::-1, ::-1], rows)
    cot_rows = jnp.swapaxes(cotangent[0], 0, 1)

    own = lax.all_to_all(fields, "sp", split_axis=2, concat_axis=1, tiled=True)
    own = jnp.swapaxes(own[0], 0, 1)
    above, below = halos(own, devices)

    def rows_spec(count):
        return pl.BlockSpec((count, GROUP, lon), lambda g: (0, g, 0))

    halo_spec = pl.BlockSpec((RIM, GROUP, above.shape[2]), lambda g: (0, g, 0))
    band_spec = pl.BlockSpec((rows, GROUP, span), lambda g: (0, g, 0))
    conv_out = pl.pallas_call(
        conv_kernel,
        name="depthwise",
        grid=(groups,),
        in_specs=[halo_spec, rows_spec(rows), halo_spec, band_spec],
        out_specs=rows_spec(rows),
        out_shape=jax.ShapeDtypeStruct((rows, channels, lon), bf16),
        scratch_shapes=[pltpu.VMEM((span, lon), bf16)],
        compiler_params=params,
    )(above, own, below, band)

    def row_spec(count):
        return pl.BlockSpec((1, count, lon), lambda h: (h, 0, 0))

    def whole(*shape):
        return pl.BlockSpec(shape, lambda h: (0,) * len(shape))

    column = lambda vector: vector[:, None]
    updated, conv_back, widen_part, narrow_part, gain_part, shift_part, hidden_part, out_part = pl.pallas_call(
        pointwise_kernel,
        name="pointwise",
        grid=(rows,),
        in_specs=[
            row_spec(channels), row_spec(channels), row_spec(channels), row_spec(1),
            whole(channels, 1), whole(channels, 1), whole(channels, wide), whole(wide, channels),
            whole(wide, 1), whole(channels, wide), whole(wide, channels), whole(channels, 1),
        ],
        out_specs=[
            row_spec(channels), row_spec(channels), whole(channels, wide), whole(channels, wide),
            whole(channels, 1), whole(channels, 1), whole(wide, 1), whole(channels, 1),
        ],
        out_shape=[
            jax.ShapeDtypeStruct((rows, channels, lon), bf16),
            jax.ShapeDtypeStruct((rows, channels, lon), bf16),
            jax.ShapeDtypeStruct((channels, wide), f32),
            jax.ShapeDtypeStruct((channels, wide), f32),
            jax.ShapeDtypeStruct((channels, 1), f32),
            jax.ShapeDtypeStruct((channels, 1), f32),
            jax.ShapeDtypeStruct((wide, 1), f32),
            jax.ShapeDtypeStruct((channels, 1), f32),
        ],
        compiler_params=params,
    )(
        conv_out, own, cot_rows, ocean_mask[:, None, :], column(norm_gain), column(norm_shift),
        widen, widen.T, column(hidden_offset), narrow, narrow.T, column(output_offset),
    )

    g_above, g_below = halos(conv_back, devices)
    pairs = pl.pallas_call(
        tap_kernel,
        name="tap_grads",
        grid=(groups,),
        in_specs=[halo_spec, rows_spec(rows), halo_spec, rows_spec(rows)],
        out_specs=pl.BlockSpec((1, 1, span), lambda g: (g, 0, 0)),
        out_shape=jax.ShapeDtypeStruct((groups, 1, span), f32),
        scratch_shapes=[pltpu.VMEM((span, lon), bf16)],
        compiler_params=params,
        cost_estimate=cost,
    )(above, own, below, conv_back)

    taps = pairs.reshape(groups, KS, rows + KS - 1, GROUP)[:, :, :KS]
    kernel_part = jnp.transpose(taps, (0, 3, 2, 1)).reshape(channels, KS * KS)
    small = jnp.concatenate([gain_part[:, 0], shift_part[:, 0], hidden_part[:, 0], out_part[:, 0]])
    pieces = [
        part.reshape(devices, -1)
        for part in (widen_part, narrow_part, jnp.pad(kernel_part, ((0, 0), (0, 128 - KS * KS))))
    ]
    pieces.append(jnp.broadcast_to(small[None], (devices, small.shape[0])))
    joined = jnp.concatenate([piece.reshape(devices, -1, 128) for piece in pieces], axis=1)
    joined = lax.all_to_all(joined, "sp", split_axis=0, concat_axis=0, tiled=True)
    summed = jnp.sum(joined, axis=0) * grad_scale

    grad_rows = pl.pallas_call(
        back_kernel,
        name="depthwise_back",
        grid=(groups,),
        in_specs=[halo_spec, rows_spec(rows), halo_spec, rows_spec(rows), band_spec],
        out_specs=rows_spec(rows),
        out_shape=jax.ShapeDtypeStruct((rows, channels, lon), bf16),
        scratch_shapes=[pltpu.VMEM((span, lon), bf16)],
        compiler_params=params,
        cost_estimate=cost,
    )(g_above, conv_back, g_below, cot_rows, band_back)

    fields_grad = lax.all_to_all(
        jnp.swapaxes(grad_rows, 0, 1)[None], "sp", split_axis=1, concat_axis=2, tiled=True
    )

    own_channels = channels // devices
    edges = np.cumsum([own_channels * wide // 128, own_channels * wide // 128, own_channels])
    widen_sum, narrow_sum, kernel_sum, small_sum = jnp.split(summed, edges)
    small_sum = small_sum.reshape(-1)
    gain_sum, shift_sum, hidden_sum, output_sum = jnp.split(small_sum, np.cumsum([channels, channels, wide]))
    return (
        jnp.swapaxes(updated, 0, 1)[None],
        fields_grad,
        kernel_sum[:, : KS * KS].reshape(-1, KS, KS),
        widen_sum.reshape(-1, wide),
        narrow_sum.reshape(-1, wide),
        gain_sum,
        shift_sum,
        hidden_sum,
        output_sum,
    )


def local(*args):
    devices = lax.axis_size("sp")
    channels, rows = args[1].shape[1:3]
    own_ch = channels // devices
    fits = own_ch * devices == channels and own_ch == 8 and rows == 4 and devices % 4 == 0 and channels == 128
    return fused(*args) if fits else stepwise(*args)


def solution(mesh):
    return jax.shard_map(
        local,
        mesh=mesh,
        in_specs=(
            P("groups", "sp", None, None),
            P("groups", None, "sp", None),
            P("sp", None),
            P("groups", None, None),
            P("groups"),
            P("groups"),
            P("groups", None),
            P("groups"),
            P("groups", None),
            P("groups"),
        ),
        out_specs=(
            P("groups", None, "sp", None),
            P("groups", "sp", None, None),
            P(("groups", "sp"), None, None),
            P(("groups", "sp"), None),
            P(("groups", "sp"), None),
            P("groups"),
            P("groups"),
            P("groups"),
            P("groups"),
        ),
        check_vma=False,
    )
```

```python
import functools
import math

import jax
import jax.numpy as jnp
import numpy as np
from jax import lax
from jax.experimental import pallas as pl
from jax.experimental.pallas import tpu as pltpu
from jax.sharding import PartitionSpec as P

KS = 7
RIM = KS // 2
EPSILON = 1e-06
GROUP = 16
NT = (((1,), (1,)), ((), ()))
TN = (((0,), (0,)), ((), ()))


def dot(former, latter):
    return jnp.dot(former, latter, preferred_element_type=jnp.float32)


def dot_nt(former, latter):
    return lax.dot_general(former, latter, NT, preferred_element_type=jnp.float32)


def dot_tn(former, latter):
    return lax.dot_general(former, latter, TN, preferred_element_type=jnp.float32)


def band_matrix(kernel, rows):
    channels = kernel.shape[0]
    taps = jnp.swapaxes(kernel, 1, 2)
    shifted = jnp.stack([jnp.pad(taps, ((0, 0), (0, 0), (h, rows - 1 - h))) for h in range(rows)])
    span = KS * (rows + KS - 1)
    shifted = shifted.reshape(rows, channels, span).astype(jnp.bfloat16)
    spread = jnp.asarray(np.repeat(np.eye(span, dtype=np.float32), GROUP, axis=1), jnp.bfloat16)
    wide = jnp.einsum("hck,kn->hcn", shifted, spread, preferred_element_type=jnp.float32)
    same = (jnp.arange(channels)[:, None] % GROUP) == (jnp.arange(span * GROUP)[None, :] % GROUP)
    return jnp.where(same[None], wide, 0.0).astype(jnp.bfloat16)


def shifts(values, scratch):
    rows, group, lon = values.shape
    flat = values.reshape(rows * group, lon)
    wrapped = jnp.concatenate([flat[:, -RIM:], flat, flat[:, :RIM]], axis=1)
    for tap in range(KS):
        scratch[tap * rows * group : (tap + 1) * rows * group, :] = wrapped[:, tap : tap + lon]


def conv_kernel(above, own, below, band, out, scratch):
    rows, group, lon = own.shape
    shifts(jnp.concatenate([above[:, :, :lon], own[...], below[:, :, :lon]], axis=0), scratch)
    result = dot(band[...].reshape(rows * group, -1), scratch[...])
    out[...] = result.astype(out.dtype).reshape(rows, group, lon)


def tap_kernel(above, own, below, grads, parts, scratch):
    rows, group, lon = own.shape
    shifts(jnp.concatenate([above[:, :, :lon], own[...], below[:, :, :lon]], axis=0), scratch)
    pairs = dot_nt(grads[...].reshape(rows * group, lon), scratch[...])
    row = lax.broadcasted_iota(jnp.int32, pairs.shape, 0) % group
    col = lax.broadcasted_iota(jnp.int32, pairs.shape, 1) % group
    kept = jnp.where(row == col, pairs, 0.0)
    total = jnp.sum(kept[:group], axis=0, keepdims=True)
    for h in range(1, rows):
        line = jnp.sum(kept[h * group : (h + 1) * group], axis=0, keepdims=True)
        total += jnp.concatenate([line[:, h * group :], line[:, : h * group]], axis=1)
    parts[...] = total[None]


def back_kernel(above, own, below, cotangent, band, out, scratch):
    rows, group, lon = own.shape
    shifts(jnp.concatenate([above[:, :, :lon], own[...], below[:, :, :lon]], axis=0), scratch)
    spread = dot(band[...].reshape(rows * group, -1), scratch[...])
    total = cotangent[...].reshape(rows * group, lon).astype(jnp.float32) + spread
    out[...] = total.astype(out.dtype).reshape(rows, group, lon)


def pointwise_kernel(
    conv, fields, cotangent, mask, gain, shift, widen, widen_t, hidden_off, narrow, narrow_t, out_off,
    updated, conv_back, widen_part, narrow_part, gain_part, shift_part, hidden_part, out_part,
):
    lon = conv.shape[-1]

    @pl.when(pl.program_id(0) == 0)
    def _():
        for part in (widen_part, narrow_part, gain_part, shift_part, hidden_part, out_part):
            part[...] = jnp.zeros_like(part)

    f32, bf16 = jnp.float32, jnp.bfloat16
    step = 256
    for first in range(0, lon, step):
        cols = slice(first, min(first + step, lon))
        values = conv[0, :, cols].astype(f32)
        centre = jnp.mean(values, axis=0, keepdims=True)
        centred = values - centre
        inv_std = lax.rsqrt(jnp.mean(centred * centred, axis=0, keepdims=True) + EPSILON)
        normed = centred * inv_std
        scaled = (normed * gain[...] + shift[...]).astype(bf16)
        hidden = dot(widen_t[...], scaled) + hidden_off[...]
        cdf = 0.5 * (1.0 + lax.erf(hidden * (1.0 / math.sqrt(2.0))))
        active = (hidden * cdf).astype(bf16)
        slope = cdf + hidden * jnp.exp(-0.5 * hidden * hidden) * (1.0 / math.sqrt(2.0 * math.pi))
        ocean = mask[0, :, cols].astype(f32)
        branch = dot(narrow[...], active) + out_off[...]
        updated[0, :, cols] = (fields[0, :, cols].astype(f32) + ocean * branch).astype(bf16)
        upstream_wide = cotangent[0, :, cols].astype(f32) * ocean
        upstream = upstream_wide.astype(bf16)
        out_part[...] += jnp.sum(upstream_wide, axis=1, keepdims=True)
        narrow_part[...] += dot_nt(upstream, active)
        hidden_wide = dot(narrow_t[...], upstream) * slope
        hidden_back = hidden_wide.astype(bf16)
        hidden_part[...] += jnp.sum(hidden_wide, axis=1, keepdims=True)
        widen_part[...] += dot_nt(scaled, hidden_back)
        scaled_back = dot(widen[...], hidden_back)
        gain_part[...] += jnp.sum(scaled_back * normed, axis=1, keepdims=True)
        shift_part[...] += jnp.sum(scaled_back, axis=1, keepdims=True)
        normed_back = scaled_back * gain[...]
        conv_back[0, :, cols] = (
            inv_std
            * (
                normed_back
                - jnp.mean(normed_back, axis=0, keepdims=True)
                - normed * jnp.mean(normed_back * normed, axis=0, keepdims=True)
            )
        ).astype(bf16)


def halos(values, devices):
    def send(piece, pairs):
        piece = jnp.pad(piece, ((0, 0), (0, 0), (0, -piece.shape[2] % 128)))
        return lax.ppermute(piece, "sp", pairs)

    above = send(values[-RIM:], [(d, d + 1) for d in range(devices - 1)])
    below = send(values[:RIM], [(d + 1, d) for d in range(devices - 1)])
    return above, below


MESH = pl.DeviceIdType.MESH
LAG = 3
EDGES = (0, 768)
STEP = 384


def eye_of(length):
    return lax.broadcasted_iota(jnp.int32, (length, length), 0) == lax.broadcasted_iota(
        jnp.int32, (length, length), 1
    )


def to_column(line):
    return jnp.sum(jnp.where(eye_of(line.shape[1]), line, 0.0), axis=1, keepdims=True)


def to_line(column):
    return jnp.sum(jnp.where(eye_of(column.shape[0]), column, 0.0), axis=0, keepdims=True)


def reorder(a, b, c):
    size = a * b * c
    out = lax.broadcasted_iota(jnp.int32, (size, size), 0)
    col = lax.broadcasted_iota(jnp.int32, (size, size), 1)
    source = ((out // c) % a) * (b * c) + (out // (a * c)) * c + out % c
    return jnp.where(source == col, 1.0, 0.0).astype(jnp.bfloat16)


def tap_spread(row, shift, rows, flip):
    tap = lax.broadcasted_iota(jnp.int32, (64, (rows + KS - 1) * GROUP), 0)
    i = lax.broadcasted_iota(jnp.int32, (64, (rows + KS - 1) * GROUP), 1) // GROUP - row
    wanted = (KS - 1 - i) * 8 + KS - 1 - shift if flip else i * 8 + shift
    return jnp.where((i >= 0) & (i < KS) & (tap == wanted), 1.0, 0.0).astype(jnp.bfloat16)


def gelu_parts(hidden):
    bell = jnp.exp(-0.5 * hidden * hidden)
    base = 1.0 + jnp.abs(hidden) * (0.3275911 / math.sqrt(2.0))
    t = pl.reciprocal(base, approx=True)
    t = t * (2.0 - base * t)
    tail = 0.5 * 1.061405429
    for factor in (-1.453152027, 1.421413741, -0.284496736, 0.254829592):
        tail = tail * t + 0.5 * factor
    tail = tail * t * bell
    cdf = jnp.where(hidden >= 0.0, 1.0 - tail, tail)
    return cdf, cdf + hidden * bell * (1.0 / math.sqrt(2.0 * math.pi))


def block_kernel(
    fields_hbm, cot_hbm, mask, kernel, gain_line, shift_line, widen, hidden_line, narrow, out_line,
    updated_hbm, fields_grad_hbm, sums,
    fields, cot_turned, cot, updated, fields_grad, taps, ocean_rows, widen_t, narrow_t,
    send, recv, own, above, below, band, band_back, wrapped, lagged, conv_out, conv_back, g_above, g_below, osend, orecv,
    weight_part, weight_send, weight_recv, rest_part, rest_recv, pairs,
    gain, shift, hidden_off, out_off, gain_part, shift_part, hidden_part, out_part,
    f_send, f_recv, h_send, h_recv, c_send, c_recv, o_send, o_recv, w_send, w_recv, t_send, t_recv, local_sem, in_sem, out_sem,
    *, devices,
):
    f32, bf16 = jnp.float32, jnp.bfloat16
    me = lax.axis_index("sp")
    rows, channels, lon = own.shape
    own_ch = fields.shape[0]
    wide = widen.shape[1]
    groups = channels // GROUP
    per_group = GROUP // own_ch
    lines = rows * own_ch
    tall = GROUP // rows
    span = band.shape[1]
    size = rows * GROUP
    wide_lon = wrapped.shape[2]
    grad_scale = 1.0 / math.sqrt(rows * devices * lon)
    turns = devices // tall

    def tall_rows(part):
        return pl.ds(pl.multiple_of(part * GROUP, GROUP), GROUP)

    def fields_in(part):
        return pltpu.make_async_copy(fields_hbm.at[:, tall_rows(part), :], fields.at[:, tall_rows(part), :], in_sem.at[part])

    def fields_out(part):
        return pltpu.make_async_copy(
            fields_grad.at[:, tall_rows(part), :], fields_grad_hbm.at[:, tall_rows(part), :], out_sem.at[part])

    cot_in = pltpu.make_async_copy(cot_hbm, cot_turned, in_sem.at[turns])
    updated_out = pltpu.make_async_copy(updated, updated_hbm, out_sem.at[turns])

    def loop(first, last, body):
        def step(k, carry):
            body(k)
            return carry

        lax.fori_loop(first, last, step, 0)

    def copy(source, target, s_sem, r_sem, device):
        return pltpu.make_async_remote_copy(
            src_ref=source, dst_ref=target, send_sem=s_sem, recv_sem=r_sem,
            device_id={"sp": device}, device_id_type=MESH,
        )

    def lanes_of(g):
        return pl.ds(pl.multiple_of(g * GROUP, GROUP), GROUP)

    loop(0, turns, lambda k: fields_in(lax.rem(me // tall + k, turns)).start())
    cot_in.start()
    barrier = pltpu.get_barrier_semaphore()
    loop(1, devices, lambda k: pl.semaphore_signal(
        barrier, inc=1, device_id={"sp": lax.rem(me + k, devices)}, device_id_type=MESH))
    pl.semaphore_wait(barrier, devices - 1)

    def f_copy(block, target):
        return copy(send.at[target], recv.at[block], f_send.at[target], f_recv.at[block], target)

    to_blocks = reorder(own_ch, tall * rows, 1)

    def pack(k):
        part = lax.rem(me // tall + k, turns)
        fields_in(part).wait()
        piece = fields[:, tall_rows(part), :].reshape(own_ch * GROUP, lon)
        moved = dot(to_blocks, piece).astype(bf16)
        send[pl.ds(part * tall, tall)] = moved.reshape(tall, lines, lon)
        for t in range(tall):
            target = part * tall + t

            @pl.when(target != me)
            def _():
                f_copy(me, target).start()

    loop(0, turns, pack)
    keep = pltpu.make_async_copy(send.at[me], recv.at[me], local_sem.at[0])
    keep.start()

    taps[...] = jnp.zeros_like(taps)
    for i in range(KS):
        taps[8 * i : 8 * i + KS, :] = kernel[i]
    weights = taps[...].astype(bf16)
    same = (lax.broadcasted_iota(jnp.int32, (channels, span), 0) % GROUP) == (
        lax.broadcasted_iota(jnp.int32, (channels, span), 1) % GROUP
    )
    for shift_at in range(KS):
        for h in range(rows):
            for flip, result in ((False, band), (True, band_back)):
                full = jnp.where(same, dot_tn(weights, tap_spread(h, shift_at, rows, flip)), 0.0).astype(bf16)
                for g in range(groups):
                    first = ((g * KS + shift_at) * rows + h) * GROUP
                    result[first : first + GROUP, :] = full[g * GROUP : (g + 1) * GROUP]
    lagged[...] = jnp.zeros_like(lagged)
    pairs[...] = jnp.zeros_like(pairs)
    gain[...] = to_column(gain_line[...])
    shift[...] = to_column(shift_line[...])
    hidden_off[...] = to_column(hidden_line[...])
    out_off[...] = to_column(out_line[...])
    for part in (weight_part, rest_part, gain_part, shift_part, hidden_part, out_part):
        part[...] = jnp.zeros_like(part)

    @pl.when(me == 0)
    def _():
        above[...] = jnp.zeros_like(above)
        g_above[...] = jnp.zeros_like(g_above)

    @pl.when(me == devices - 1)
    def _():
        below[...] = jnp.zeros_like(below)
        g_below[...] = jnp.zeros_like(g_below)

    one_hot = jnp.where(eye_of(wide), 1.0, 0.0).astype(bf16)
    turn = one_hot[:channels, :channels]
    for r in range(rows):
        ocean_rows[r] = mask[r : r + 1, :].astype(f32)
    widen_t[...] = dot_nt(one_hot, widen[...]).astype(bf16)
    narrow_t[...] = dot_nt(one_hot, narrow[...]).astype(bf16)
    cot_in.wait()

    def turn_cot(r):
        cot[r] = dot_nt(turn, cot_turned[r]).astype(bf16)

    loop(0, rows, turn_cot)
    keep.wait()

    def down_copy(g):
        return copy(own.at[rows - RIM : rows, lanes_of(g), :], above.at[:, lanes_of(g), :],
                    h_send.at[g], h_recv.at[g], me + 1)

    def up_copy(g):
        return copy(own.at[0:RIM, lanes_of(g), :], below.at[:, lanes_of(g), :],
                    h_send.at[groups + g], h_recv.at[groups + g], me - 1)

    to_rows = reorder(per_group, rows, own_ch)
    to_owners = reorder(rows, per_group, own_ch)
    my_group = me // per_group

    def group_at(k):
        return lax.rem(my_group + groups - k, groups)

    def receive(g):
        for t in range(per_group):
            source = g * per_group + t

            @pl.when(source != me)
            def _():
                f_copy(source, source).wait_recv()

        pair = recv[pl.ds(g * per_group, per_group)].reshape(per_group * lines, lon)
        own[:, lanes_of(g), :] = dot(to_rows, pair).astype(bf16).reshape(rows, GROUP, lon)

        @pl.when(me < devices - 1)
        def _():
            down_copy(g).start()

        @pl.when(me > 0)
        def _():
            up_copy(g).start()

    def spread_dot(ref, g, values, width):
        terms = dot(ref[pl.ds(pl.multiple_of(g * KS * size, KS * size), KS * size), :], values)
        total = terms[:size, :width]
        for shift_at in range(1, KS):
            total = total + terms[shift_at * size : (shift_at + 1) * size, shift_at : shift_at + width]
        return total

    def conv(g):
        @pl.when(me > 0)
        def _():
            copy(above.at[:, lanes_of(g), :], above.at[:, lanes_of(g), :],
                 h_send.at[g], h_recv.at[g], me - 1).wait_recv()

        @pl.when(me < devices - 1)
        def _():
            copy(below.at[:, lanes_of(g), :], below.at[:, lanes_of(g), :],
                 h_send.at[groups + g], h_recv.at[groups + g], me + 1).wait_recv()

        flat = jnp.concatenate([above[:, lanes_of(g), :], own[:, lanes_of(g), :], below[:, lanes_of(g), :]], axis=0)
        flat = flat.reshape(span, lon)
        filler = jnp.zeros((span, wide_lon - lon - 2 * RIM), bf16)
        wrapped[g] = jnp.concatenate([flat[:, -RIM:], flat, flat[:, :RIM], filler], axis=1)
        conv_out[:, lanes_of(g), :] = spread_dot(band, g, wrapped[g], lon).astype(bf16).reshape(rows, GROUP, lon)

    def forward(k):
        @pl.when(k < groups)
        def _():
            receive(group_at(k))

        @pl.when(k >= LAG)
        def _():
            conv(group_at(lax.rem(k - LAG + 1, groups)))

    loop(0, groups + LAG, forward)

    edges = [min(edge, lon) for edge in EDGES if edge < lon] + [lon]
    pieces = list(zip(edges[:-1], edges[1:]))
    ranges = [[(max(first - 128, 128), last - 128)] for first, last in pieces]
    ranges[-1] = [(ranges[-1][0][0], lon), (0, 128)]
    spans = [part for parts in ranges for part in parts]

    def row_down(k):
        cols = pl.ds(pieces[k][0], pieces[k][1] - pieces[k][0])
        return copy(conv_back.at[rows - RIM : rows, :, cols], g_above.at[:, :, cols], c_send.at[k], c_recv.at[k], me + 1)

    def row_up(k):
        cols = pl.ds(pieces[k][0], pieces[k][1] - pieces[k][0])
        at = len(pieces) + k
        return copy(conv_back.at[0:RIM, :, cols], g_below.at[:, :, cols], c_send.at[at], c_recv.at[at], me - 1)

    def pointwise(r, start, end):
        step = STEP
        for first in range(start, end, step):
            cols = slice(first, min(first + step, end))
            values = conv_out[r, :, cols].astype(f32)
            centre = jnp.mean(values, axis=0, keepdims=True)
            centred = values - centre
            inv_std = lax.rsqrt(jnp.mean(centred * centred, axis=0, keepdims=True) + EPSILON)
            normed = centred * inv_std
            scaled = (normed * gain[...] + shift[...]).astype(bf16)
            hidden = dot(widen_t[...], scaled) + hidden_off[...]
            cdf, slope = gelu_parts(hidden)
            active = (hidden * cdf).astype(bf16)
            ocean = ocean_rows[r, :, cols]
            branch = dot(narrow[...], active) + out_off[...]
            fresh = (own[r, :, cols].astype(f32) + ocean * branch).astype(bf16)
            for at in range(0, cols.stop - first, 128):
                end_at = min(at + 128, cols.stop - first)
                turned = dot_nt(one_hot[: end_at - at, : end_at - at], fresh[:, at:end_at])
                updated[r, first + at : first + end_at, :] = turned.astype(bf16)
            upstream_wide = cot[r, :, cols].astype(f32) * ocean
            upstream = upstream_wide.astype(bf16)
            out_part[...] += jnp.sum(upstream_wide, axis=1, keepdims=True)
            weight_part[:, wide:] += dot_nt(upstream, active)
            hidden_wide = dot(narrow_t[...], upstream) * slope
            hidden_back = hidden_wide.astype(bf16)
            found = dot_nt(jnp.concatenate([scaled, jnp.ones((16, scaled.shape[1]), bf16)], axis=0), hidden_back)
            weight_part[:, :wide] += found[:channels]
            hidden_part[...] += found[channels:]
            scaled_back = dot(widen[...], hidden_back)
            gain_part[...] += jnp.sum(scaled_back * normed, axis=1, keepdims=True)
            shift_part[...] += jnp.sum(scaled_back, axis=1, keepdims=True)
            normed_back = scaled_back * gain[...]
            conv_back[r, :, cols] = (
                inv_std
                * (
                    normed_back
                    - jnp.mean(normed_back, axis=0, keepdims=True)
                    - normed * jnp.mean(normed_back * normed, axis=0, keepdims=True)
                )
            ).astype(bf16)

    def piece(k):
        loop(0, rows, lambda r: pointwise(r, *pieces[k]))

        @pl.when(me < devices - 1)
        def _():
            row_down(k).start()

        @pl.when(me > 0)
        def _():
            row_up(k).start()

    def w_copy(block, target):
        return copy(weight_send.at[target], weight_recv.at[block], w_send.at[target], w_recv.at[block], target)

    def others(body):
        loop(1, devices, lambda k: body(lax.rem(me + k, devices)))

    def send_weights():
        for d in range(devices):
            at = slice(d * own_ch, (d + 1) * own_ch)
            weight_send[d] = jnp.concatenate([weight_part[at, :wide], weight_part[at, wide:]], axis=0).astype(bf16)
        others(lambda d: w_copy(me, d).start())

    diagonal = (lax.broadcasted_iota(jnp.int32, (KS * size, span), 0) % GROUP) == (
        lax.broadcasted_iota(jnp.int32, (KS * size, span), 1) % GROUP
    )

    def tap(g):
        values = conv_back[:, lanes_of(g), :].reshape(size, lon)
        for shift_at in range(KS):
            block = values
            if shift_at:
                block = jnp.concatenate([jnp.zeros((size, shift_at), bf16), values], axis=1)
            lagged[shift_at * size : (shift_at + 1) * size, : lon + shift_at] = block
        kept = jnp.where(diagonal, dot_nt(lagged[...], wrapped[g]), 0.0)
        for shift_at in range(KS):
            total = kept[shift_at * size : shift_at * size + GROUP, : KS * GROUP]
            for h in range(1, rows):
                first = shift_at * size + h * GROUP
                total = total + kept[first : first + GROUP, h * GROUP : (h + KS) * GROUP]
            pairs[shift_at, lanes_of(g), : KS * GROUP] = total

    def o_copy(at, block, target):
        cols = pl.ds(spans[at][0], spans[at][1] - spans[at][0])
        return copy(osend.at[target, :, cols], orecv.at[block, :, cols], o_send.at[at, target], o_recv.at[at, block], target)

    def window(ref, g, first, last):
        left = ref[:, lanes_of(g), first - 128 : first] if first else ref[:, lanes_of(g), lon - lon % 128 - 128 * (lon % 128 == 0) : lon]
        right = ref[:, lanes_of(g), last : min(last + 128, lon)] if last < lon else ref[:, lanes_of(g), :128]
        return jnp.concatenate([left[:, :, -RIM:], ref[:, lanes_of(g), first:last], right[:, :, :RIM]], axis=2)

    def back(g, at):
        first, last = spans[at]
        values = jnp.concatenate([window(ref, g, first, last) for ref in (g_above, conv_back, g_below)], axis=0)
        total = cot[:, lanes_of(g), first:last].reshape(size, last - first).astype(f32) + spread_dot(
            band_back, g, values.reshape(span, last - first + 2 * RIM), last - first)
        moved = dot(to_owners, total.astype(bf16)).astype(bf16)
        osend[pl.ds(g * per_group, per_group), :, first:last] = moved.reshape(per_group, lines, last - first)
        for t in range(per_group):
            target = g * per_group + t

            @pl.when(target != me)
            def _():
                o_copy(at, me, target).start()

    def back_piece(k):
        cols = pl.ds(pieces[k][0], pieces[k][1] - pieces[k][0])

        @pl.when(me > 0)
        def _():
            copy(g_above.at[:, :, cols], g_above.at[:, :, cols], c_send.at[k], c_recv.at[k], me - 1).wait_recv()

        @pl.when(me < devices - 1)
        def _():
            at = len(pieces) + k
            copy(g_below.at[:, :, cols], g_below.at[:, :, cols], c_send.at[at], c_recv.at[at], me + 1).wait_recv()

        for part in ranges[k]:
            at = spans.index(part)
            loop(0, groups, lambda j: back(lax.rem(my_group + groups // 2 + j, groups), at))

    ahead = 2
    for k in range(len(pieces)):
        piece(k)
        if k >= ahead:
            back_piece(k - ahead)
    updated_out.start()
    send_weights()
    rest = list(range(max(len(pieces) - ahead, 0), len(pieces)))
    done = 0
    for k in rest:
        until = min(done + 2, groups)
        loop(done, until, tap)
        done = until
        back_piece(k)
    own_back = pltpu.make_async_copy(osend.at[me], orecv.at[me], local_sem.at[1])
    own_back.start()
    loop(done, groups, tap)

    found = jnp.zeros((channels, 64), f32)
    line_at = lax.broadcasted_iota(jnp.int32, (128, 64), 0) // GROUP
    tap_at = lax.broadcasted_iota(jnp.int32, (128, 64), 1)
    for shift_at in range(KS):
        spread = jnp.where(tap_at == line_at * 8 + shift_at, 1.0, 0.0).astype(bf16)
        exact = pairs[shift_at]
        high = exact.astype(bf16)
        low = (exact - high.astype(f32)).astype(bf16)
        found = found + dot(high, spread) + dot(low, spread)
    rest_part[:, :64] = found
    small = jnp.concatenate(
        [to_line(gain_part[...]), to_line(shift_part[...])]
        + [hidden_part[:1, first : first + 128] for first in range(0, wide, 128)]
        + [to_line(out_part[...])], axis=0)
    for d in range(devices):
        rest_part[d * own_ch : d * own_ch + small.shape[0], 128:] = small

    def t_copy(block, target):
        return copy(rest_part.at[pl.ds(pl.multiple_of(target * own_ch, own_ch), own_ch), :],
                    rest_recv.at[block], t_send.at[target], t_recv.at[block], target)

    others(lambda d: t_copy(me, d).start())

    own_back.wait()
    from_blocks = reorder(tall * rows, own_ch, 1)

    def unpack(k):
        part = lax.rem(me // tall + k, turns)
        for t in range(tall):
            source = part * tall + t

            @pl.when(source != me)
            def _():
                for at in range(len(spans)):
                    o_copy(at, source, source).wait_recv()

        moved = dot(from_blocks, orecv[pl.ds(part * tall, tall)].reshape(tall * lines, lon)).astype(bf16)
        fields_grad[:, tall_rows(part), :] = moved.reshape(own_ch, GROUP, lon)
        fields_out(part).start()

    loop(0, turns, unpack)

    mine = pl.ds(pl.multiple_of(me * own_ch, own_ch), own_ch)
    weight_recv[pl.ds(me, 1)] = weight_send[pl.ds(me, 1)]
    rest_recv[pl.ds(me, 1)] = rest_part[mine, :][None]
    others(lambda d: w_copy(d, d).wait_recv())
    others(lambda d: t_copy(d, d).wait_recv())
    weight_sum = jnp.sum(weight_recv[...].astype(f32), axis=0) * grad_scale
    sums[: 2 * own_ch, :] = weight_sum
    sums[2 * own_ch :, :] = jnp.sum(rest_recv[...], axis=0) * grad_scale

    others(lambda d: f_copy(me, d).wait_send())
    for at in range(len(spans)):
        others(lambda d: o_copy(at, me, d).wait_send())
    others(lambda d: w_copy(me, d).wait_send())
    others(lambda d: t_copy(me, d).wait_send())

    @pl.when(me < devices - 1)
    def _():
        loop(0, groups, lambda g: down_copy(g).wait_send())
        for k in range(len(pieces)):
            row_down(k).wait_send()

    @pl.when(me > 0)
    def _():
        loop(0, groups, lambda g: up_copy(g).wait_send())
        for k in range(len(pieces)):
            row_up(k).wait_send()

    updated_out.wait()
    loop(0, turns, lambda part: fields_out(part).wait())


def finish_kernel(sums, kernel_grad, widen_grad, narrow_grad, gain_grad, shift_grad, hidden_grad, out_grad):
    own_ch, wide = widen_grad.shape
    first = 2 * own_ch
    widen_grad[...] = sums[:own_ch, :]
    narrow_grad[...] = sums[own_ch:first, :]
    for i in range(KS):
        kernel_grad[i] = sums[first:, 8 * i : 8 * i + KS]
    gain_grad[...] = sums[first : first + 1, 128:]
    shift_grad[...] = sums[first + 1 : first + 2, 128:]
    for line in range(wide // 128):
        hidden_grad[:, line * 128 : (line + 1) * 128] = sums[first + 2 + line : first + 3 + line, 128:]
    out_grad[...] = sums[first + 2 + wide // 128 : first + 3 + wide // 128, 128:]


def fused(
    fields, cotangent, ocean_mask, kernel, norm_gain, norm_shift, widen, hidden_offset, narrow, output_offset
):
    devices = lax.axis_size("sp")
    _, channels, rows, lon = cotangent.shape
    own_ch = channels // devices
    wide = widen.shape[1]
    groups = channels // GROUP
    span = (rows + KS - 1) * GROUP
    wide_lon = -(-(lon + 2 * RIM) // 128) * 128
    f32, bf16 = jnp.float32, jnp.bfloat16
    line = lambda vector: vector[None, :]
    vmem = pl.BlockSpec(memory_space=pltpu.VMEM)
    dma = pltpu.SemaphoreType.DMA
    hbm = pl.BlockSpec(memory_space=pl.ANY)
    shape = jax.ShapeDtypeStruct
    pieces = len([edge for edge in EDGES if edge < lon])
    turns = devices * rows // GROUP
    updated, fields_grad, sums = pl.pallas_call(
        functools.partial(block_kernel, devices=devices),
        name="block",
        in_specs=[hbm, hbm] + [vmem] * 8,
        out_specs=[hbm, hbm, vmem],
        out_shape=[
            shape((rows, lon, channels), bf16),
            shape((own_ch, rows * devices, lon), bf16),
            shape((3 * own_ch, wide), f32),
        ],
        scratch_shapes=[
            pltpu.VMEM((own_ch, rows * devices, lon), bf16),
            pltpu.VMEM((rows, lon, channels), bf16),
            pltpu.VMEM((rows, channels, lon), bf16),
            pltpu.VMEM((rows, lon, channels), bf16),
            pltpu.VMEM((own_ch, rows * devices, lon), bf16),
            pltpu.VMEM((64, channels), f32),
            pltpu.VMEM((rows, 1, lon), f32),
            pltpu.VMEM((wide, channels), bf16),
            pltpu.VMEM((wide, channels), bf16),
            pltpu.VMEM((devices, rows * own_ch, lon), bf16),
            pltpu.VMEM((devices, rows * own_ch, lon), bf16),
            pltpu.VMEM((rows, channels, lon), bf16),
            pltpu.VMEM((RIM, channels, lon), bf16),
            pltpu.VMEM((RIM, channels, lon), bf16),
            pltpu.VMEM((groups * KS * rows * GROUP, span), bf16),
            pltpu.VMEM((groups * KS * rows * GROUP, span), bf16),
            pltpu.VMEM((groups, span, wide_lon), bf16),
            pltpu.VMEM((KS * rows * GROUP, wide_lon), bf16),
            pltpu.VMEM((rows, channels, lon), bf16),
            pltpu.VMEM((rows, channels, lon), bf16),
            pltpu.VMEM((RIM, channels, lon), bf16),
            pltpu.VMEM((RIM, channels, lon), bf16),
            pltpu.VMEM((devices, rows * own_ch, lon), bf16),
            pltpu.VMEM((devices, rows * own_ch, lon), bf16),
            pltpu.VMEM((channels, 2 * wide), f32),
            pltpu.VMEM((devices, 2 * own_ch, wide), bf16),
            pltpu.VMEM((devices, 2 * own_ch, wide), bf16),
            pltpu.VMEM((channels, 256), f32),
            pltpu.VMEM((devices, own_ch, 256), f32),
            pltpu.VMEM((KS, channels, 128), f32),
            pltpu.VMEM((channels, 1), f32),
            pltpu.VMEM((channels, 1), f32),
            pltpu.VMEM((wide, 1), f32),
            pltpu.VMEM((channels, 1), f32),
            pltpu.VMEM((channels, 1), f32),
            pltpu.VMEM((channels, 1), f32),
            pltpu.VMEM((16, wide), f32),
            pltpu.VMEM((channels, 1), f32),
            dma((devices,)), dma((devices,)),
            dma((2 * groups,)), dma((2 * groups,)),
            dma((2 * pieces,)), dma((2 * pieces,)),
            dma((pieces + 1, devices)), dma((pieces + 1, devices)),
            dma((devices,)), dma((devices,)),
            dma((devices,)), dma((devices,)),
            dma((2,)), dma((turns + 1,)), dma((turns + 1,)),
        ],
        compiler_params=pltpu.CompilerParams(
            collective_id=0, has_side_effects=True, vmem_limit_bytes=56 * 1024 * 1024
        ),
        cost_estimate=pl.CostEstimate(
            flops=6 * KS * rows * GROUP * span * lon * groups, bytes_accessed=12 * rows * channels * lon,
            transcendentals=0,
        ),
    )(
        fields[0], jnp.transpose(cotangent[0], (1, 2, 0)), ocean_mask, jnp.transpose(kernel, (1, 2, 0)),
        line(norm_gain), line(norm_shift), widen, line(hidden_offset), narrow, line(output_offset),
    )
    kernel_grad, widen_grad, narrow_grad, gain_grad, shift_grad, hidden_grad, out_grad = pl.pallas_call(
        finish_kernel,
        name="finish",
        in_specs=[vmem],
        out_specs=[vmem] * 7,
        out_shape=[
            shape((KS, own_ch, KS), f32),
            shape((own_ch, wide), f32),
            shape((own_ch, wide), f32),
            shape((1, channels), f32),
            shape((1, channels), f32),
            shape((1, wide), f32),
            shape((1, channels), f32),
        ],
    )(sums)
    return (
        jnp.transpose(updated, (2, 0, 1))[None],
        fields_grad[None],
        jnp.transpose(kernel_grad, (1, 0, 2)),
        widen_grad,
        narrow_grad,
        gain_grad[0],
        shift_grad[0],
        hidden_grad[0],
        out_grad[0],
    )


def stepwise(
    fields, cotangent, ocean_mask, kernel, norm_gain, norm_shift, widen, hidden_offset, narrow, output_offset
):
    devices = lax.axis_size("sp")
    samples, channels, rows, lon = cotangent.shape
    wide = widen.shape[1]
    f32, bf16 = jnp.float32, jnp.bfloat16
    grad_scale = 1.0 / math.sqrt(samples * rows * devices * lon)
    groups = channels // GROUP
    span = KS * (rows + KS - 1) * GROUP
    cost = pl.CostEstimate(
        flops=20 * rows * GROUP * span * lon * groups, bytes_accessed=4 * rows * channels * lon * 3, transcendentals=0
    )
    params = pltpu.CompilerParams(vmem_limit_bytes=48 * 1024 * 1024)

    band = band_matrix(kernel, rows)
    band_back = band_matrix(kernel[:, ::-1, ::-1], rows)
    cot_rows = jnp.swapaxes(cotangent[0], 0, 1)

    own = lax.all_to_all(fields, "sp", split_axis=2, concat_axis=1, tiled=True)
    own = jnp.swapaxes(own[0], 0, 1)
    above, below = halos(own, devices)

    def rows_spec(count):
        return pl.BlockSpec((count, GROUP, lon), lambda g: (0, g, 0))

    halo_spec = pl.BlockSpec((RIM, GROUP, above.shape[2]), lambda g: (0, g, 0))
    band_spec = pl.BlockSpec((rows, GROUP, span), lambda g: (0, g, 0))
    conv_out = pl.pallas_call(
        conv_kernel,
        name="depthwise",
        grid=(groups,),
        in_specs=[halo_spec, rows_spec(rows), halo_spec, band_spec],
        out_specs=rows_spec(rows),
        out_shape=jax.ShapeDtypeStruct((rows, channels, lon), bf16),
        scratch_shapes=[pltpu.VMEM((span, lon), bf16)],
        compiler_params=params,
    )(above, own, below, band)

    def row_spec(count):
        return pl.BlockSpec((1, count, lon), lambda h: (h, 0, 0))

    def whole(*shape):
        return pl.BlockSpec(shape, lambda h: (0,) * len(shape))

    column = lambda vector: vector[:, None]
    updated, conv_back, widen_part, narrow_part, gain_part, shift_part, hidden_part, out_part = pl.pallas_call(
        pointwise_kernel,
        name="pointwise",
        grid=(rows,),
        in_specs=[
            row_spec(channels), row_spec(channels), row_spec(channels), row_spec(1),
            whole(channels, 1), whole(channels, 1), whole(channels, wide), whole(wide, channels),
            whole(wide, 1), whole(channels, wide), whole(wide, channels), whole(channels, 1),
        ],
        out_specs=[
            row_spec(channels), row_spec(channels), whole(channels, wide), whole(channels, wide),
            whole(channels, 1), whole(channels, 1), whole(wide, 1), whole(channels, 1),
        ],
        out_shape=[
            jax.ShapeDtypeStruct((rows, channels, lon), bf16),
            jax.ShapeDtypeStruct((rows, channels, lon), bf16),
            jax.ShapeDtypeStruct((channels, wide), f32),
            jax.ShapeDtypeStruct((channels, wide), f32),
            jax.ShapeDtypeStruct((channels, 1), f32),
            jax.ShapeDtypeStruct((channels, 1), f32),
            jax.ShapeDtypeStruct((wide, 1), f32),
            jax.ShapeDtypeStruct((channels, 1), f32),
        ],
        compiler_params=params,
    )(
        conv_out, own, cot_rows, ocean_mask[:, None, :], column(norm_gain), column(norm_shift),
        widen, widen.T, column(hidden_offset), narrow, narrow.T, column(output_offset),
    )

    g_above, g_below = halos(conv_back, devices)
    pairs = pl.pallas_call(
        tap_kernel,
        name="tap_grads",
        grid=(groups,),
        in_specs=[halo_spec, rows_spec(rows), halo_spec, rows_spec(rows)],
        out_specs=pl.BlockSpec((1, 1, span), lambda g: (g, 0, 0)),
        out_shape=jax.ShapeDtypeStruct((groups, 1, span), f32),
        scratch_shapes=[pltpu.VMEM((span, lon), bf16)],
        compiler_params=params,
        cost_estimate=cost,
    )(above, own, below, conv_back)

    taps = pairs.reshape(groups, KS, rows + KS - 1, GROUP)[:, :, :KS]
    kernel_part = jnp.transpose(taps, (0, 3, 2, 1)).reshape(channels, KS * KS)
    small = jnp.concatenate([gain_part[:, 0], shift_part[:, 0], hidden_part[:, 0], out_part[:, 0]])
    pieces = [
        part.reshape(devices, -1)
        for part in (widen_part, narrow_part, jnp.pad(kernel_part, ((0, 0), (0, 128 - KS * KS))))
    ]
    pieces.append(jnp.broadcast_to(small[None], (devices, small.shape[0])))
    joined = jnp.concatenate([piece.reshape(devices, -1, 128) for piece in pieces], axis=1)
    joined = lax.all_to_all(joined, "sp", split_axis=0, concat_axis=0, tiled=True)
    summed = jnp.sum(joined, axis=0) * grad_scale

    grad_rows = pl.pallas_call(
        back_kernel,
        name="depthwise_back",
        grid=(groups,),
        in_specs=[halo_spec, rows_spec(rows), halo_spec, rows_spec(rows), band_spec],
        out_specs=rows_spec(rows),
        out_shape=jax.ShapeDtypeStruct((rows, channels, lon), bf16),
        scratch_shapes=[pltpu.VMEM((span, lon), bf16)],
        compiler_params=params,
        cost_estimate=cost,
    )(g_above, conv_back, g_below, cot_rows, band_back)

    fields_grad = lax.all_to_all(
        jnp.swapaxes(grad_rows, 0, 1)[None], "sp", split_axis=1, concat_axis=2, tiled=True
    )

    own_channels = channels // devices
    edges = np.cumsum([own_channels * wide // 128, own_channels * wide // 128, own_channels])
    widen_sum, narrow_sum, kernel_sum, small_sum = jnp.split(summed, edges)
    small_sum = small_sum.reshape(-1)
    gain_sum, shift_sum, hidden_sum, output_sum = jnp.split(small_sum, np.cumsum([channels, channels, wide]))
    return (
        jnp.swapaxes(updated, 0, 1)[None],
        fields_grad,
        kernel_sum[:, : KS * KS].reshape(-1, KS, KS),
        widen_sum.reshape(-1, wide),
        narrow_sum.reshape(-1, wide),
        gain_sum,
        shift_sum,
        hidden_sum,
        output_sum,
    )


def local(*args):
    devices = lax.axis_size("sp")
    channels, rows = args[1].shape[1:3]
    own_ch = channels // devices
    fits = own_ch * devices == channels and own_ch == 8 and rows == 4 and devices % 4 == 0 and channels == 128
    return fused(*args) if fits else stepwise(*args)


def solution(mesh):
    return jax.shard_map(
        local,
        mesh=mesh,
        in_specs=(
            P("groups", "sp", None, None),
            P("groups", None, "sp", None),
            P("sp", None),
            P("groups", None, None),
            P("groups"),
            P("groups"),
            P("groups", None),
            P("groups"),
            P("groups", None),
            P("groups"),
        ),
        out_specs=(
            P("groups", None, "sp", None),
            P("groups", "sp", None, None),
            P(("groups", "sp"), None, None),
            P(("groups", "sp"), None),
            P(("groups", "sp"), None),
            P("groups"),
            P("groups"),
            P("groups"),
            P("groups"),
        ),
        check_vma=False,
    )
```

```python
import functools
import math

import jax
import jax.numpy as jnp
import numpy as np
from jax import lax
from jax.experimental import pallas as pl
from jax.experimental.pallas import tpu as pltpu
from jax.sharding import PartitionSpec as P

KS = 7
RIM = KS // 2
EPSILON = 1e-06
GROUP = 16
NT = (((1,), (1,)), ((), ()))
TN = (((0,), (0,)), ((), ()))


def dot(former, latter):
    return jnp.dot(former, latter, preferred_element_type=jnp.float32)


def dot_nt(former, latter):
    return lax.dot_general(former, latter, NT, preferred_element_type=jnp.float32)


def dot_tn(former, latter):
    return lax.dot_general(former, latter, TN, preferred_element_type=jnp.float32)


def band_matrix(kernel, rows):
    channels = kernel.shape[0]
    taps = jnp.swapaxes(kernel, 1, 2)
    shifted = jnp.stack([jnp.pad(taps, ((0, 0), (0, 0), (h, rows - 1 - h))) for h in range(rows)])
    span = KS * (rows + KS - 1)
    shifted = shifted.reshape(rows, channels, span).astype(jnp.bfloat16)
    spread = jnp.asarray(np.repeat(np.eye(span, dtype=np.float32), GROUP, axis=1), jnp.bfloat16)
    wide = jnp.einsum("hck,kn->hcn", shifted, spread, preferred_element_type=jnp.float32)
    same = (jnp.arange(channels)[:, None] % GROUP) == (jnp.arange(span * GROUP)[None, :] % GROUP)
    return jnp.where(same[None], wide, 0.0).astype(jnp.bfloat16)


def shifts(values, scratch):
    rows, group, lon = values.shape
    flat = values.reshape(rows * group, lon)
    wrapped = jnp.concatenate([flat[:, -RIM:], flat, flat[:, :RIM]], axis=1)
    for tap in range(KS):
        scratch[tap * rows * group : (tap + 1) * rows * group, :] = wrapped[:, tap : tap + lon]


def conv_kernel(above, own, below, band, out, scratch):
    rows, group, lon = own.shape
    shifts(jnp.concatenate([above[:, :, :lon], own[...], below[:, :, :lon]], axis=0), scratch)
    result = dot(band[...].reshape(rows * group, -1), scratch[...])
    out[...] = result.astype(out.dtype).reshape(rows, group, lon)


def tap_kernel(above, own, below, grads, parts, scratch):
    rows, group, lon = own.shape
    shifts(jnp.concatenate([above[:, :, :lon], own[...], below[:, :, :lon]], axis=0), scratch)
    pairs = dot_nt(grads[...].reshape(rows * group, lon), scratch[...])
    row = lax.broadcasted_iota(jnp.int32, pairs.shape, 0) % group
    col = lax.broadcasted_iota(jnp.int32, pairs.shape, 1) % group
    kept = jnp.where(row == col, pairs, 0.0)
    total = jnp.sum(kept[:group], axis=0, keepdims=True)
    for h in range(1, rows):
        line = jnp.sum(kept[h * group : (h + 1) * group], axis=0, keepdims=True)
        total += jnp.concatenate([line[:, h * group :], line[:, : h * group]], axis=1)
    parts[...] = total[None]


def back_kernel(above, own, below, cotangent, band, out, scratch):
    rows, group, lon = own.shape
    shifts(jnp.concatenate([above[:, :, :lon], own[...], below[:, :, :lon]], axis=0), scratch)
    spread = dot(band[...].reshape(rows * group, -1), scratch[...])
    total = cotangent[...].reshape(rows * group, lon).astype(jnp.float32) + spread
    out[...] = total.astype(out.dtype).reshape(rows, group, lon)


def pointwise_kernel(
    conv, fields, cotangent, mask, gain, shift, widen, widen_t, hidden_off, narrow, narrow_t, out_off,
    updated, conv_back, widen_part, narrow_part, gain_part, shift_part, hidden_part, out_part,
):
    lon = conv.shape[-1]

    @pl.when(pl.program_id(0) == 0)
    def _():
        for part in (widen_part, narrow_part, gain_part, shift_part, hidden_part, out_part):
            part[...] = jnp.zeros_like(part)

    f32, bf16 = jnp.float32, jnp.bfloat16
    step = 256
    for first in range(0, lon, step):
        cols = slice(first, min(first + step, lon))
        values = conv[0, :, cols].astype(f32)
        centre = jnp.mean(values, axis=0, keepdims=True)
        centred = values - centre
        inv_std = lax.rsqrt(jnp.mean(centred * centred, axis=0, keepdims=True) + EPSILON)
        normed = centred * inv_std
        scaled = (normed * gain[...] + shift[...]).astype(bf16)
        hidden = dot(widen_t[...], scaled) + hidden_off[...]
        cdf = 0.5 * (1.0 + lax.erf(hidden * (1.0 / math.sqrt(2.0))))
        active = (hidden * cdf).astype(bf16)
        slope = cdf + hidden * jnp.exp(-0.5 * hidden * hidden) * (1.0 / math.sqrt(2.0 * math.pi))
        ocean = mask[0, :, cols].astype(f32)
        branch = dot(narrow[...], active) + out_off[...]
        updated[0, :, cols] = (fields[0, :, cols].astype(f32) + ocean * branch).astype(bf16)
        upstream_wide = cotangent[0, :, cols].astype(f32) * ocean
        upstream = upstream_wide.astype(bf16)
        out_part[...] += jnp.sum(upstream_wide, axis=1, keepdims=True)
        narrow_part[...] += dot_nt(upstream, active)
        hidden_wide = dot(narrow_t[...], upstream) * slope
        hidden_back = hidden_wide.astype(bf16)
        hidden_part[...] += jnp.sum(hidden_wide, axis=1, keepdims=True)
        widen_part[...] += dot_nt(scaled, hidden_back)
        scaled_back = dot(widen[...], hidden_back)
        gain_part[...] += jnp.sum(scaled_back * normed, axis=1, keepdims=True)
        shift_part[...] += jnp.sum(scaled_back, axis=1, keepdims=True)
        normed_back = scaled_back * gain[...]
        conv_back[0, :, cols] = (
            inv_std
            * (
                normed_back
                - jnp.mean(normed_back, axis=0, keepdims=True)
                - normed * jnp.mean(normed_back * normed, axis=0, keepdims=True)
            )
        ).astype(bf16)


def halos(values, devices):
    def send(piece, pairs):
        piece = jnp.pad(piece, ((0, 0), (0, 0), (0, -piece.shape[2] % 128)))
        return lax.ppermute(piece, "sp", pairs)

    above = send(values[-RIM:], [(d, d + 1) for d in range(devices - 1)])
    below = send(values[:RIM], [(d + 1, d) for d in range(devices - 1)])
    return above, below


MESH = pl.DeviceIdType.MESH
LAG = 3
EDGES = (0, 384, 896)
STEP = 384


def eye_of(length):
    return lax.broadcasted_iota(jnp.int32, (length, length), 0) == lax.broadcasted_iota(
        jnp.int32, (length, length), 1
    )


def to_column(line):
    return jnp.sum(jnp.where(eye_of(line.shape[1]), line, 0.0), axis=1, keepdims=True)


def to_line(column):
    return jnp.sum(jnp.where(eye_of(column.shape[0]), column, 0.0), axis=0, keepdims=True)


def reorder(a, b, c):
    size = a * b * c
    out = lax.broadcasted_iota(jnp.int32, (size, size), 0)
    col = lax.broadcasted_iota(jnp.int32, (size, size), 1)
    source = ((out // c) % a) * (b * c) + (out // (a * c)) * c + out % c
    return jnp.where(source == col, 1.0, 0.0).astype(jnp.bfloat16)


def tap_spread(row, shift, rows, flip):
    tap = lax.broadcasted_iota(jnp.int32, (64, (rows + KS - 1) * GROUP), 0)
    i = lax.broadcasted_iota(jnp.int32, (64, (rows + KS - 1) * GROUP), 1) // GROUP - row
    wanted = (KS - 1 - i) * 8 + KS - 1 - shift if flip else i * 8 + shift
    return jnp.where((i >= 0) & (i < KS) & (tap == wanted), 1.0, 0.0).astype(jnp.bfloat16)


def gelu_parts(hidden):
    bell = jnp.exp(-0.5 * hidden * hidden)
    base = 1.0 + jnp.abs(hidden) * (0.3275911 / math.sqrt(2.0))
    t = pl.reciprocal(base, approx=True)
    t = t * (2.0 - base * t)
    tail = 0.5 * 1.061405429
    for factor in (-1.453152027, 1.421413741, -0.284496736, 0.254829592):
        tail = tail * t + 0.5 * factor
    tail = tail * t * bell
    cdf = jnp.where(hidden >= 0.0, 1.0 - tail, tail)
    return cdf, cdf + hidden * bell * (1.0 / math.sqrt(2.0 * math.pi))


def block_kernel(
    fields_hbm, cot_hbm, mask, kernel, gain_line, shift_line, widen, hidden_line, narrow, out_line,
    updated_hbm, fields_grad_hbm, sums,
    fields, cot_turned, cot, updated, fields_grad, taps, ocean_rows, widen_t, narrow_t,
    send, recv, own, above, below, band, band_back, wrapped, lagged, conv_out, conv_back, g_above, g_below, osend, orecv,
    weight_part, weight_send, weight_recv, rest_part, rest_recv, pairs,
    gain, shift, hidden_off, out_off, gain_part, shift_part, hidden_part, out_part,
    f_send, f_recv, h_send, h_recv, c_send, c_recv, o_send, o_recv, w_send, w_recv, t_send, t_recv, local_sem, in_sem, out_sem,
    *, devices,
):
    f32, bf16 = jnp.float32, jnp.bfloat16
    me = lax.axis_index("sp")
    rows, channels, lon = own.shape
    own_ch = fields.shape[0]
    wide = widen.shape[1]
    groups = channels // GROUP
    per_group = GROUP // own_ch
    lines = rows * own_ch
    tall = GROUP // rows
    span = band.shape[1]
    size = rows * GROUP
    wide_lon = wrapped.shape[2]
    grad_scale = 1.0 / math.sqrt(rows * devices * lon)
    turns = devices // tall

    def tall_rows(part):
        return pl.ds(pl.multiple_of(part * GROUP, GROUP), GROUP)

    def fields_in(part):
        return pltpu.make_async_copy(fields_hbm.at[:, tall_rows(part), :], fields.at[:, tall_rows(part), :], in_sem.at[part])

    def fields_out(part):
        return pltpu.make_async_copy(
            fields_grad.at[:, tall_rows(part), :], fields_grad_hbm.at[:, tall_rows(part), :], out_sem.at[part])

    cot_in = pltpu.make_async_copy(cot_hbm, cot_turned, in_sem.at[turns])
    updated_out = pltpu.make_async_copy(updated, updated_hbm, out_sem.at[turns])

    def loop(first, last, body):
        def step(k, carry):
            body(k)
            return carry

        lax.fori_loop(first, last, step, 0)

    def copy(source, target, s_sem, r_sem, device):
        return pltpu.make_async_remote_copy(
            src_ref=source, dst_ref=target, send_sem=s_sem, recv_sem=r_sem,
            device_id={"sp": device}, device_id_type=MESH,
        )

    def lanes_of(g):
        return pl.ds(pl.multiple_of(g * GROUP, GROUP), GROUP)

    loop(0, turns, lambda k: fields_in(lax.rem(me // tall + k, turns)).start())
    cot_in.start()
    barrier = pltpu.get_barrier_semaphore()
    loop(1, devices, lambda k: pl.semaphore_signal(
        barrier, inc=1, device_id={"sp": lax.rem(me + k, devices)}, device_id_type=MESH))
    pl.semaphore_wait(barrier, devices - 1)

    def f_copy(block, target):
        return copy(send.at[target], recv.at[block], f_send.at[target], f_recv.at[block], target)

    to_blocks = reorder(own_ch, tall * rows, 1)

    def pack(k):
        part = lax.rem(me // tall + k, turns)
        fields_in(part).wait()
        piece = fields[:, tall_rows(part), :].reshape(own_ch * GROUP, lon)
        moved = dot(to_blocks, piece).astype(bf16)
        send[pl.ds(part * tall, tall)] = moved.reshape(tall, lines, lon)
        for t in range(tall):
            target = part * tall + t

            @pl.when(target != me)
            def _():
                f_copy(me, target).start()

    loop(0, turns, pack)
    keep = pltpu.make_async_copy(send.at[me], recv.at[me], local_sem.at[0])
    keep.start()

    taps[...] = jnp.zeros_like(taps)
    for i in range(KS):
        taps[8 * i : 8 * i + KS, :] = kernel[i]
    weights = taps[...].astype(bf16)
    same = (lax.broadcasted_iota(jnp.int32, (channels, span), 0) % GROUP) == (
        lax.broadcasted_iota(jnp.int32, (channels, span), 1) % GROUP
    )
    for shift_at in range(KS):
        for h in range(rows):
            for flip, result in ((False, band), (True, band_back)):
                full = jnp.where(same, dot_tn(weights, tap_spread(h, shift_at, rows, flip)), 0.0).astype(bf16)
                for g in range(groups):
                    first = ((g * KS + shift_at) * rows + h) * GROUP
                    result[first : first + GROUP, :] = full[g * GROUP : (g + 1) * GROUP]
    lagged[...] = jnp.zeros_like(lagged)
    pairs[...] = jnp.zeros_like(pairs)
    gain[...] = to_column(gain_line[...])
    shift[...] = to_column(shift_line[...])
    hidden_off[...] = to_column(hidden_line[...])
    out_off[...] = to_column(out_line[...])
    for part in (weight_part, rest_part, gain_part, shift_part, hidden_part, out_part):
        part[...] = jnp.zeros_like(part)

    @pl.when(me == 0)
    def _():
        above[...] = jnp.zeros_like(above)
        g_above[...] = jnp.zeros_like(g_above)

    @pl.when(me == devices - 1)
    def _():
        below[...] = jnp.zeros_like(below)
        g_below[...] = jnp.zeros_like(g_below)

    one_hot = jnp.where(eye_of(wide), 1.0, 0.0).astype(bf16)
    turn = one_hot[:channels, :channels]
    for r in range(rows):
        ocean_rows[r] = mask[r : r + 1, :].astype(f32)
    widen_t[...] = dot_nt(one_hot, widen[...]).astype(bf16)
    narrow_t[...] = dot_nt(one_hot, narrow[...]).astype(bf16)
    cot_in.wait()

    def turn_cot(r):
        cot[r] = dot_nt(turn, cot_turned[r]).astype(bf16)

    loop(0, rows, turn_cot)
    keep.wait()

    def down_copy(g):
        return copy(own.at[rows - RIM : rows, lanes_of(g), :], above.at[:, lanes_of(g), :],
                    h_send.at[g], h_recv.at[g], me + 1)

    def up_copy(g):
        return copy(own.at[0:RIM, lanes_of(g), :], below.at[:, lanes_of(g), :],
                    h_send.at[groups + g], h_recv.at[groups + g], me - 1)

    to_rows = reorder(per_group, rows, own_ch)
    to_owners = reorder(rows, per_group, own_ch)
    my_group = me // per_group

    def group_at(k):
        return lax.rem(my_group + groups - k, groups)

    def receive(g):
        for t in range(per_group):
            source = g * per_group + t

            @pl.when(source != me)
            def _():
                f_copy(source, source).wait_recv()

        pair = recv[pl.ds(g * per_group, per_group)].reshape(per_group * lines, lon)
        own[:, lanes_of(g), :] = dot(to_rows, pair).astype(bf16).reshape(rows, GROUP, lon)

        @pl.when(me < devices - 1)
        def _():
            down_copy(g).start()

        @pl.when(me > 0)
        def _():
            up_copy(g).start()

    def spread_dot(ref, g, values, width):
        terms = dot(ref[pl.ds(pl.multiple_of(g * KS * size, KS * size), KS * size), :], values)
        total = terms[:size, :width]
        for shift_at in range(1, KS):
            total = total + terms[shift_at * size : (shift_at + 1) * size, shift_at : shift_at + width]
        return total

    def conv(g):
        @pl.when(me > 0)
        def _():
            copy(above.at[:, lanes_of(g), :], above.at[:, lanes_of(g), :],
                 h_send.at[g], h_recv.at[g], me - 1).wait_recv()

        @pl.when(me < devices - 1)
        def _():
            copy(below.at[:, lanes_of(g), :], below.at[:, lanes_of(g), :],
                 h_send.at[groups + g], h_recv.at[groups + g], me + 1).wait_recv()

        flat = jnp.concatenate([above[:, lanes_of(g), :], own[:, lanes_of(g), :], below[:, lanes_of(g), :]], axis=0)
        flat = flat.reshape(span, lon)
        filler = jnp.zeros((span, wide_lon - lon - 2 * RIM), bf16)
        wrapped[g] = jnp.concatenate([flat[:, -RIM:], flat, flat[:, :RIM], filler], axis=1)
        conv_out[:, lanes_of(g), :] = spread_dot(band, g, wrapped[g], lon).astype(bf16).reshape(rows, GROUP, lon)

    def forward(k):
        @pl.when(k < groups)
        def _():
            receive(group_at(k))

        @pl.when(k >= LAG)
        def _():
            conv(group_at(lax.rem(k - LAG + 1, groups)))

    loop(0, groups + LAG, forward)

    edges = [min(edge, lon) for edge in EDGES if edge < lon] + [lon]
    pieces = list(zip(edges[:-1], edges[1:]))
    ranges = [[(max(first - 128, 128), last - 128)] for first, last in pieces]
    ranges[-1] = [(ranges[-1][0][0], lon), (0, 128)]
    spans = [part for parts in ranges for part in parts]

    def row_down(k):
        cols = pl.ds(pieces[k][0], pieces[k][1] - pieces[k][0])
        return copy(conv_back.at[rows - RIM : rows, :, cols], g_above.at[:, :, cols], c_send.at[k], c_recv.at[k], me + 1)

    def row_up(k):
        cols = pl.ds(pieces[k][0], pieces[k][1] - pieces[k][0])
        at = len(pieces) + k
        return copy(conv_back.at[0:RIM, :, cols], g_below.at[:, :, cols], c_send.at[at], c_recv.at[at], me - 1)

    def pointwise(r, start, end):
        step = STEP
        for first in range(start, end, step):
            cols = slice(first, min(first + step, end))
            values = conv_out[r, :, cols].astype(f32)
            centre = jnp.mean(values, axis=0, keepdims=True)
            centred = values - centre
            inv_std = lax.rsqrt(jnp.mean(centred * centred, axis=0, keepdims=True) + EPSILON)
            normed = centred * inv_std
            scaled = (normed * gain[...] + shift[...]).astype(bf16)
            hidden = dot(widen_t[...], scaled) + hidden_off[...]
            cdf, slope = gelu_parts(hidden)
            active = (hidden * cdf).astype(bf16)
            ocean = ocean_rows[r, :, cols]
            branch = dot(narrow[...], active) + out_off[...]
            fresh = (own[r, :, cols].astype(f32) + ocean * branch).astype(bf16)
            conv_out[r, :, cols] = fresh
            upstream_wide = cot[r, :, cols].astype(f32) * ocean
            upstream = upstream_wide.astype(bf16)
            out_part[...] += jnp.sum(upstream_wide, axis=1, keepdims=True)
            weight_part[:, wide:] += dot_nt(upstream, active)
            hidden_wide = dot(narrow_t[...], upstream) * slope
            hidden_back = hidden_wide.astype(bf16)
            found = dot_nt(jnp.concatenate([scaled, jnp.ones((16, scaled.shape[1]), bf16)], axis=0), hidden_back)
            weight_part[:, :wide] += found[:channels]
            hidden_part[...] += found[channels:]
            scaled_back = dot(widen[...], hidden_back)
            gain_part[...] += jnp.sum(scaled_back * normed, axis=1, keepdims=True)
            shift_part[...] += jnp.sum(scaled_back, axis=1, keepdims=True)
            normed_back = scaled_back * gain[...]
            conv_back[r, :, cols] = (
                inv_std
                * (
                    normed_back
                    - jnp.mean(normed_back, axis=0, keepdims=True)
                    - normed * jnp.mean(normed_back * normed, axis=0, keepdims=True)
                )
            ).astype(bf16)

    def piece(k):
        loop(0, rows, lambda r: pointwise(r, *pieces[k]))

        @pl.when(me < devices - 1)
        def _():
            row_down(k).start()

        @pl.when(me > 0)
        def _():
            row_up(k).start()

    def w_copy(block, target):
        return copy(weight_send.at[target], weight_recv.at[block], w_send.at[target], w_recv.at[block], target)

    def others(body):
        loop(1, devices, lambda k: body(lax.rem(me + k, devices)))

    def send_weights():
        for d in range(devices):
            at = slice(d * own_ch, (d + 1) * own_ch)
            weight_send[d] = jnp.concatenate([weight_part[at, :wide], weight_part[at, wide:]], axis=0).astype(bf16)
        others(lambda d: w_copy(me, d).start())

    diagonal = (lax.broadcasted_iota(jnp.int32, (KS * size, span), 0) % GROUP) == (
        lax.broadcasted_iota(jnp.int32, (KS * size, span), 1) % GROUP
    )

    def tap(g):
        values = conv_back[:, lanes_of(g), :].reshape(size, lon)
        for shift_at in range(KS):
            block = values
            if shift_at:
                block = jnp.concatenate([jnp.zeros((size, shift_at), bf16), values], axis=1)
            lagged[shift_at * size : (shift_at + 1) * size, : lon + shift_at] = block
        kept = jnp.where(diagonal, dot_nt(lagged[...], wrapped[g]), 0.0)
        for shift_at in range(KS):
            total = kept[shift_at * size : shift_at * size + GROUP, : KS * GROUP]
            for h in range(1, rows):
                first = shift_at * size + h * GROUP
                total = total + kept[first : first + GROUP, h * GROUP : (h + KS) * GROUP]
            pairs[shift_at, lanes_of(g), : KS * GROUP] = total

    def o_copy(at, block, target):
        cols = pl.ds(spans[at][0], spans[at][1] - spans[at][0])
        return copy(osend.at[target, :, cols], orecv.at[block, :, cols], o_send.at[at, target], o_recv.at[at, block], target)

    def window(ref, g, first, last):
        left = ref[:, lanes_of(g), first - 128 : first] if first else ref[:, lanes_of(g), lon - lon % 128 - 128 * (lon % 128 == 0) : lon]
        right = ref[:, lanes_of(g), last : min(last + 128, lon)] if last < lon else ref[:, lanes_of(g), :128]
        return jnp.concatenate([left[:, :, -RIM:], ref[:, lanes_of(g), first:last], right[:, :, :RIM]], axis=2)

    def back(g, at):
        first, last = spans[at]
        values = jnp.concatenate([window(ref, g, first, last) for ref in (g_above, conv_back, g_below)], axis=0)
        total = cot[:, lanes_of(g), first:last].reshape(size, last - first).astype(f32) + spread_dot(
            band_back, g, values.reshape(span, last - first + 2 * RIM), last - first)
        moved = dot(to_owners, total.astype(bf16)).astype(bf16)
        osend[pl.ds(g * per_group, per_group), :, first:last] = moved.reshape(per_group, lines, last - first)
        for t in range(per_group):
            target = g * per_group + t

            @pl.when(target != me)
            def _():
                o_copy(at, me, target).start()

    def back_piece(k):
        cols = pl.ds(pieces[k][0], pieces[k][1] - pieces[k][0])

        @pl.when(me > 0)
        def _():
            copy(g_above.at[:, :, cols], g_above.at[:, :, cols], c_send.at[k], c_recv.at[k], me - 1).wait_recv()

        @pl.when(me < devices - 1)
        def _():
            at = len(pieces) + k
            copy(g_below.at[:, :, cols], g_below.at[:, :, cols], c_send.at[at], c_recv.at[at], me + 1).wait_recv()

        for part in ranges[k]:
            at = spans.index(part)
            loop(0, groups, lambda j: back(lax.rem(my_group + groups // 2 + j, groups), at))

    ahead = 2
    for k in range(len(pieces)):
        piece(k)
        if k >= ahead:
            back_piece(k - ahead)
    send_weights()
    rest = list(range(max(len(pieces) - ahead, 0), len(pieces)))
    done = 0
    for k in rest:
        until = min(done + 2, groups)
        loop(done, until, tap)
        done = until
        back_piece(k)
    own_back = pltpu.make_async_copy(osend.at[me], orecv.at[me], local_sem.at[1])
    own_back.start()
    loop(done, groups, tap)

    def turn_updated(r):
        for first in range(0, lon, 128):
            last = min(first + 128, lon)
            fresh = conv_out[r, :, first:last]
            updated[r, first:last, :] = dot_nt(one_hot[: last - first, : last - first], fresh).astype(bf16)

    loop(0, rows, turn_updated)
    updated_out.start()

    found = jnp.zeros((channels, 64), f32)
    line_at = lax.broadcasted_iota(jnp.int32, (128, 64), 0) // GROUP
    tap_at = lax.broadcasted_iota(jnp.int32, (128, 64), 1)
    for shift_at in range(KS):
        spread = jnp.where(tap_at == line_at * 8 + shift_at, 1.0, 0.0).astype(bf16)
        exact = pairs[shift_at]
        high = exact.astype(bf16)
        low = (exact - high.astype(f32)).astype(bf16)
        found = found + dot(high, spread) + dot(low, spread)
    rest_part[:, :64] = found
    small = jnp.concatenate(
        [to_line(gain_part[...]), to_line(shift_part[...])]
        + [hidden_part[:1, first : first + 128] for first in range(0, wide, 128)]
        + [to_line(out_part[...])], axis=0)
    for d in range(devices):
        rest_part[d * own_ch : d * own_ch + small.shape[0], 128:] = small

    def t_copy(block, target):
        return copy(rest_part.at[pl.ds(pl.multiple_of(target * own_ch, own_ch), own_ch), :],
                    rest_recv.at[block], t_send.at[target], t_recv.at[block], target)

    others(lambda d: t_copy(me, d).start())

    own_back.wait()
    from_blocks = reorder(tall * rows, own_ch, 1)

    def unpack(k):
        part = lax.rem(me // tall + k, turns)
        for t in range(tall):
            source = part * tall + t

            @pl.when(source != me)
            def _():
                for at in range(len(spans)):
                    o_copy(at, source, source).wait_recv()

        moved = dot(from_blocks, orecv[pl.ds(part * tall, tall)].reshape(tall * lines, lon)).astype(bf16)
        fields_grad[:, tall_rows(part), :] = moved.reshape(own_ch, GROUP, lon)
        fields_out(part).start()

    loop(0, turns, unpack)

    mine = pl.ds(pl.multiple_of(me * own_ch, own_ch), own_ch)
    weight_recv[pl.ds(me, 1)] = weight_send[pl.ds(me, 1)]
    rest_recv[pl.ds(me, 1)] = rest_part[mine, :][None]
    others(lambda d: w_copy(d, d).wait_recv())
    others(lambda d: t_copy(d, d).wait_recv())
    weight_sum = jnp.sum(weight_recv[...].astype(f32), axis=0) * grad_scale
    sums[: 2 * own_ch, :] = weight_sum
    sums[2 * own_ch :, :] = jnp.sum(rest_recv[...], axis=0) * grad_scale

    others(lambda d: f_copy(me, d).wait_send())
    for at in range(len(spans)):
        others(lambda d: o_copy(at, me, d).wait_send())
    others(lambda d: w_copy(me, d).wait_send())
    others(lambda d: t_copy(me, d).wait_send())

    @pl.when(me < devices - 1)
    def _():
        loop(0, groups, lambda g: down_copy(g).wait_send())
        for k in range(len(pieces)):
            row_down(k).wait_send()

    @pl.when(me > 0)
    def _():
        loop(0, groups, lambda g: up_copy(g).wait_send())
        for k in range(len(pieces)):
            row_up(k).wait_send()

    updated_out.wait()
    loop(0, turns, lambda part: fields_out(part).wait())


def finish_kernel(sums, kernel_grad, widen_grad, narrow_grad, gain_grad, shift_grad, hidden_grad, out_grad):
    own_ch, wide = widen_grad.shape
    first = 2 * own_ch
    widen_grad[...] = sums[:own_ch, :]
    narrow_grad[...] = sums[own_ch:first, :]
    for i in range(KS):
        kernel_grad[i] = sums[first:, 8 * i : 8 * i + KS]
    gain_grad[...] = sums[first : first + 1, 128:]
    shift_grad[...] = sums[first + 1 : first + 2, 128:]
    for line in range(wide // 128):
        hidden_grad[:, line * 128 : (line + 1) * 128] = sums[first + 2 + line : first + 3 + line, 128:]
    out_grad[...] = sums[first + 2 + wide // 128 : first + 3 + wide // 128, 128:]


def fused(
    fields, cotangent, ocean_mask, kernel, norm_gain, norm_shift, widen, hidden_offset, narrow, output_offset
):
    devices = lax.axis_size("sp")
    _, channels, rows, lon = cotangent.shape
    own_ch = channels // devices
    wide = widen.shape[1]
    groups = channels // GROUP
    span = (rows + KS - 1) * GROUP
    wide_lon = -(-(lon + 2 * RIM) // 128) * 128
    f32, bf16 = jnp.float32, jnp.bfloat16
    line = lambda vector: vector[None, :]
    vmem = pl.BlockSpec(memory_space=pltpu.VMEM)
    dma = pltpu.SemaphoreType.DMA
    hbm = pl.BlockSpec(memory_space=pl.ANY)
    shape = jax.ShapeDtypeStruct
    pieces = len([edge for edge in EDGES if edge < lon])
    turns = devices * rows // GROUP
    updated, fields_grad, sums = pl.pallas_call(
        functools.partial(block_kernel, devices=devices),
        name="block",
        in_specs=[hbm, hbm] + [vmem] * 8,
        out_specs=[hbm, hbm, vmem],
        out_shape=[
            shape((rows, lon, channels), bf16),
            shape((own_ch, rows * devices, lon), bf16),
            shape((3 * own_ch, wide), f32),
        ],
        scratch_shapes=[
            pltpu.VMEM((own_ch, rows * devices, lon), bf16),
            pltpu.VMEM((rows, lon, channels), bf16),
            pltpu.VMEM((rows, channels, lon), bf16),
            pltpu.VMEM((rows, lon, channels), bf16),
            pltpu.VMEM((own_ch, rows * devices, lon), bf16),
            pltpu.VMEM((64, channels), f32),
            pltpu.VMEM((rows, 1, lon), f32),
            pltpu.VMEM((wide, channels), bf16),
            pltpu.VMEM((wide, channels), bf16),
            pltpu.VMEM((devices, rows * own_ch, lon), bf16),
            pltpu.VMEM((devices, rows * own_ch, lon), bf16),
            pltpu.VMEM((rows, channels, lon), bf16),
            pltpu.VMEM((RIM, channels, lon), bf16),
            pltpu.VMEM((RIM, channels, lon), bf16),
            pltpu.VMEM((groups * KS * rows * GROUP, span), bf16),
            pltpu.VMEM((groups * KS * rows * GROUP, span), bf16),
            pltpu.VMEM((groups, span, wide_lon), bf16),
            pltpu.VMEM((KS * rows * GROUP, wide_lon), bf16),
            pltpu.VMEM((rows, channels, lon), bf16),
            pltpu.VMEM((rows, channels, lon), bf16),
            pltpu.VMEM((RIM, channels, lon), bf16),
            pltpu.VMEM((RIM, channels, lon), bf16),
            pltpu.VMEM((devices, rows * own_ch, lon), bf16),
            pltpu.VMEM((devices, rows * own_ch, lon), bf16),
            pltpu.VMEM((channels, 2 * wide), f32),
            pltpu.VMEM((devices, 2 * own_ch, wide), bf16),
            pltpu.VMEM((devices, 2 * own_ch, wide), bf16),
            pltpu.VMEM((channels, 256), f32),
            pltpu.VMEM((devices, own_ch, 256), f32),
            pltpu.VMEM((KS, channels, 128), f32),
            pltpu.VMEM((channels, 1), f32),
            pltpu.VMEM((channels, 1), f32),
            pltpu.VMEM((wide, 1), f32),
            pltpu.VMEM((channels, 1), f32),
            pltpu.VMEM((channels, 1), f32),
            pltpu.VMEM((channels, 1), f32),
            pltpu.VMEM((16, wide), f32),
            pltpu.VMEM((channels, 1), f32),
            dma((devices,)), dma((devices,)),
            dma((2 * groups,)), dma((2 * groups,)),
            dma((2 * pieces,)), dma((2 * pieces,)),
            dma((pieces + 1, devices)), dma((pieces + 1, devices)),
            dma((devices,)), dma((devices,)),
            dma((devices,)), dma((devices,)),
            dma((2,)), dma((turns + 1,)), dma((turns + 1,)),
        ],
        compiler_params=pltpu.CompilerParams(
            collective_id=0, has_side_effects=True, vmem_limit_bytes=56 * 1024 * 1024
        ),
        cost_estimate=pl.CostEstimate(
            flops=6 * KS * rows * GROUP * span * lon * groups, bytes_accessed=12 * rows * channels * lon,
            transcendentals=0,
        ),
    )(
        fields[0], jnp.transpose(cotangent[0], (1, 2, 0)), ocean_mask, jnp.transpose(kernel, (1, 2, 0)),
        line(norm_gain), line(norm_shift), widen, line(hidden_offset), narrow, line(output_offset),
    )
    kernel_grad, widen_grad, narrow_grad, gain_grad, shift_grad, hidden_grad, out_grad = pl.pallas_call(
        finish_kernel,
        name="finish",
        in_specs=[vmem],
        out_specs=[vmem] * 7,
        out_shape=[
            shape((KS, own_ch, KS), f32),
            shape((own_ch, wide), f32),
            shape((own_ch, wide), f32),
            shape((1, channels), f32),
            shape((1, channels), f32),
            shape((1, wide), f32),
            shape((1, channels), f32),
        ],
    )(sums)
    return (
        jnp.transpose(updated, (2, 0, 1))[None],
        fields_grad[None],
        jnp.transpose(kernel_grad, (1, 0, 2)),
        widen_grad,
        narrow_grad,
        gain_grad[0],
        shift_grad[0],
        hidden_grad[0],
        out_grad[0],
    )


def stepwise(
    fields, cotangent, ocean_mask, kernel, norm_gain, norm_shift, widen, hidden_offset, narrow, output_offset
):
    devices = lax.axis_size("sp")
    samples, channels, rows, lon = cotangent.shape
    wide = widen.shape[1]
    f32, bf16 = jnp.float32, jnp.bfloat16
    grad_scale = 1.0 / math.sqrt(samples * rows * devices * lon)
    groups = channels // GROUP
    span = KS * (rows + KS - 1) * GROUP
    cost = pl.CostEstimate(
        flops=20 * rows * GROUP * span * lon * groups, bytes_accessed=4 * rows * channels * lon * 3, transcendentals=0
    )
    params = pltpu.CompilerParams(vmem_limit_bytes=48 * 1024 * 1024)

    band = band_matrix(kernel, rows)
    band_back = band_matrix(kernel[:, ::-1, ::-1], rows)
    cot_rows = jnp.swapaxes(cotangent[0], 0, 1)

    own = lax.all_to_all(fields, "sp", split_axis=2, concat_axis=1, tiled=True)
    own = jnp.swapaxes(own[0], 0, 1)
    above, below = halos(own, devices)

    def rows_spec(count):
        return pl.BlockSpec((count, GROUP, lon), lambda g: (0, g, 0))

    halo_spec = pl.BlockSpec((RIM, GROUP, above.shape[2]), lambda g: (0, g, 0))
    band_spec = pl.BlockSpec((rows, GROUP, span), lambda g: (0, g, 0))
    conv_out = pl.pallas_call(
        conv_kernel,
        name="depthwise",
        grid=(groups,),
        in_specs=[halo_spec, rows_spec(rows), halo_spec, band_spec],
        out_specs=rows_spec(rows),
        out_shape=jax.ShapeDtypeStruct((rows, channels, lon), bf16),
        scratch_shapes=[pltpu.VMEM((span, lon), bf16)],
        compiler_params=params,
    )(above, own, below, band)

    def row_spec(count):
        return pl.BlockSpec((1, count, lon), lambda h: (h, 0, 0))

    def whole(*shape):
        return pl.BlockSpec(shape, lambda h: (0,) * len(shape))

    column = lambda vector: vector[:, None]
    updated, conv_back, widen_part, narrow_part, gain_part, shift_part, hidden_part, out_part = pl.pallas_call(
        pointwise_kernel,
        name="pointwise",
        grid=(rows,),
        in_specs=[
            row_spec(channels), row_spec(channels), row_spec(channels), row_spec(1),
            whole(channels, 1), whole(channels, 1), whole(channels, wide), whole(wide, channels),
            whole(wide, 1), whole(channels, wide), whole(wide, channels), whole(channels, 1),
        ],
        out_specs=[
            row_spec(channels), row_spec(channels), whole(channels, wide), whole(channels, wide),
            whole(channels, 1), whole(channels, 1), whole(wide, 1), whole(channels, 1),
        ],
        out_shape=[
            jax.ShapeDtypeStruct((rows, channels, lon), bf16),
            jax.ShapeDtypeStruct((rows, channels, lon), bf16),
            jax.ShapeDtypeStruct((channels, wide), f32),
            jax.ShapeDtypeStruct((channels, wide), f32),
            jax.ShapeDtypeStruct((channels, 1), f32),
            jax.ShapeDtypeStruct((channels, 1), f32),
            jax.ShapeDtypeStruct((wide, 1), f32),
            jax.ShapeDtypeStruct((channels, 1), f32),
        ],
        compiler_params=params,
    )(
        conv_out, own, cot_rows, ocean_mask[:, None, :], column(norm_gain), column(norm_shift),
        widen, widen.T, column(hidden_offset), narrow, narrow.T, column(output_offset),
    )

    g_above, g_below = halos(conv_back, devices)
    pairs = pl.pallas_call(
        tap_kernel,
        name="tap_grads",
        grid=(groups,),
        in_specs=[halo_spec, rows_spec(rows), halo_spec, rows_spec(rows)],
        out_specs=pl.BlockSpec((1, 1, span), lambda g: (g, 0, 0)),
        out_shape=jax.ShapeDtypeStruct((groups, 1, span), f32),
        scratch_shapes=[pltpu.VMEM((span, lon), bf16)],
        compiler_params=params,
        cost_estimate=cost,
    )(above, own, below, conv_back)

    taps = pairs.reshape(groups, KS, rows + KS - 1, GROUP)[:, :, :KS]
    kernel_part = jnp.transpose(taps, (0, 3, 2, 1)).reshape(channels, KS * KS)
    small = jnp.concatenate([gain_part[:, 0], shift_part[:, 0], hidden_part[:, 0], out_part[:, 0]])
    pieces = [
        part.reshape(devices, -1)
        for part in (widen_part, narrow_part, jnp.pad(kernel_part, ((0, 0), (0, 128 - KS * KS))))
    ]
    pieces.append(jnp.broadcast_to(small[None], (devices, small.shape[0])))
    joined = jnp.concatenate([piece.reshape(devices, -1, 128) for piece in pieces], axis=1)
    joined = lax.all_to_all(joined, "sp", split_axis=0, concat_axis=0, tiled=True)
    summed = jnp.sum(joined, axis=0) * grad_scale

    grad_rows = pl.pallas_call(
        back_kernel,
        name="depthwise_back",
        grid=(groups,),
        in_specs=[halo_spec, rows_spec(rows), halo_spec, rows_spec(rows), band_spec],
        out_specs=rows_spec(rows),
        out_shape=jax.ShapeDtypeStruct((rows, channels, lon), bf16),
        scratch_shapes=[pltpu.VMEM((span, lon), bf16)],
        compiler_params=params,
        cost_estimate=cost,
    )(g_above, conv_back, g_below, cot_rows, band_back)

    fields_grad = lax.all_to_all(
        jnp.swapaxes(grad_rows, 0, 1)[None], "sp", split_axis=1, concat_axis=2, tiled=True
    )

    own_channels = channels // devices
    edges = np.cumsum([own_channels * wide // 128, own_channels * wide // 128, own_channels])
    widen_sum, narrow_sum, kernel_sum, small_sum = jnp.split(summed, edges)
    small_sum = small_sum.reshape(-1)
    gain_sum, shift_sum, hidden_sum, output_sum = jnp.split(small_sum, np.cumsum([channels, channels, wide]))
    return (
        jnp.swapaxes(updated, 0, 1)[None],
        fields_grad,
        kernel_sum[:, : KS * KS].reshape(-1, KS, KS),
        widen_sum.reshape(-1, wide),
        narrow_sum.reshape(-1, wide),
        gain_sum,
        shift_sum,
        hidden_sum,
        output_sum,
    )


def local(*args):
    devices = lax.axis_size("sp")
    channels, rows = args[1].shape[1:3]
    own_ch = channels // devices
    fits = own_ch * devices == channels and own_ch == 8 and rows == 4 and devices % 4 == 0 and channels == 128
    return fused(*args) if fits else stepwise(*args)


def solution(mesh):
    return jax.shard_map(
        local,
        mesh=mesh,
        in_specs=(
            P("groups", "sp", None, None),
            P("groups", None, "sp", None),
            P("sp", None),
            P("groups", None, None),
            P("groups"),
            P("groups"),
            P("groups", None),
            P("groups"),
            P("groups", None),
            P("groups"),
        ),
        out_specs=(
            P("groups", None, "sp", None),
            P("groups", "sp", None, None),
            P(("groups", "sp"), None, None),
            P(("groups", "sp"), None),
            P(("groups", "sp"), None),
            P("groups"),
            P("groups"),
            P("groups"),
            P("groups"),
        ),
        check_vma=False,
    )
```
